32 devices in a mesh: grp: 2 (over x), seq: 16 (over z, y, core).
Axes of the slice: x: 2, y: 2, z: 4, core: 2. Of those that a mesh axis runs over, the one named last changes fastest.
Arguments:
- queries: bfloat16 [128, 5120], P(('grp', 'seq')), parts along dimension 0
- keys: bfloat16 [16384, 5120], P(('grp', 'seq')), parts along dimension 0
- values: bfloat16 [16384, 5120], P(('grp', 'seq')), parts along dimension 0, may hold values from -6 to 6
- gain: float32 [5120], replicated, may hold values from 0.1 to 1.9
Outputs:
- window_out: bfloat16 [128, 5120], P(('grp', 'seq')), parts along dimension 0
The draws below stay inside these ranges and needn't reach their ends.
There are 2 independent parts, one for each index of `grp`. The reference program is written for one: setup_inputs(seed, part) draws one part's arguments, and reference() takes and returns one part's arrays. A program takes and returns all parts, laid end to end along the dimension named above; an argument that names none is the same for every part. Nothing has to cross between parts.
All inputs are finite; a program needn't handle non-finite values.
Results may differ from the reference program's by a relative error of at most 0.001.
Values may be sent and summed in bfloat16 or wider, within the bound.
No kernel may reach another device: no remote copies, remote signals or barrier semaphores. Data moves between devices by JAX's collectives and lax.ppermute only.
A program may use at most 128 MiB of HBM per device.

```python
import math
import jax
import jax.numpy as jnp
from jax import lax

HEADS = 40
HDIM = 128
HD = 5120
TOKENS = 8192
QW = 64


def base_keys(key):
    return jnp.clip(jax.random.normal(jax.random.fold_in(key, 11), (TOKENS, HD), jnp.float32), -6.0, 6.0)


def draw_keys(key, part):
    result = base_keys(key)
    return result.astype(jnp.bfloat16)


def draw_queries(key, part):
    result = 1.5 * jnp.clip(jax.random.normal(jax.random.fold_in(key, 17), (QW, HD), jnp.float32), -6.0, 6.0)
    return result.astype(jnp.bfloat16)


def levels(rng, shape, shards, smallest, largest):
    def one(position, blocks):
        steps = jax.random.uniform(jax.random.fold_in(jax.random.fold_in(rng, 6), position), (blocks,), jnp.float32, smallest / len(shards), largest / len(shards))
        return jnp.repeat(jnp.exp(steps), shape[position] // blocks).reshape((-1,) + (1,) * (len(shape) - position - 1))

    factor_of = one(*shards[0])
    for cut in shards[1:]:
        factor_of = factor_of * one(*cut)
    return factor_of


def normal_values(rng, dims, scale, bound, cuts=(), kind=jnp.bfloat16):
    values = jax.random.normal(rng, dims, jnp.float32) * scale
    if len(cuts) > 0:
        values = levels(rng, dims, cuts, -0.22, 0.18) * values
    return jnp.clip(values, min=-bound, max=bound).astype(kind)


def setup_inputs(seed: int = 0, part: int = 0) -> dict:
    key_list = jax.random.split(jax.random.key(seed), 5)
    part_keys = jax.random.split(jax.random.fold_in(key_list[4], part), 5)
    queries = draw_queries(jax.random.fold_in(jax.random.fold_in(key_list[4], part), 71), part)
    keys = draw_keys(jax.random.fold_in(jax.random.fold_in(key_list[4], part), 71), part)
    values = normal_values(part_keys[2], (TOKENS, HD), 1.0, 6.0, ((0, 16),))
    gain = jnp.clip(1.0 + 0.18 * jax.random.normal(key_list[3], (HD,), jnp.float32), 0.1, 1.9)
    return dict(queries=queries, keys=keys, values=values, gain=gain)


def reference(queries, keys, values, gain):
    score_scale = 1.0 / math.sqrt(HDIM)
    query_heads = queries.reshape(QW, HEADS, HDIM).transpose(1, 0, 2)
    key_heads = keys.reshape(TOKENS, HEADS, HDIM).transpose(1, 0, 2)
    value_heads = values.reshape(TOKENS, HEADS, HDIM).transpose(1, 0, 2)

    def one_head(members):
        query_head, key_head, value_head = members
        scores = jnp.dot(query_head, key_head.T, preferred_element_type=jnp.float32) * score_scale
        row_max = lax.optimization_barrier(jnp.max(scores, axis=1, keepdims=True))
        weights = jnp.exp(scores - row_max)
        denominator = lax.optimization_barrier(jnp.sum(weights, axis=1, keepdims=True))
        numerator = jnp.dot(weights, value_head.astype(jnp.float32), precision=lax.Precision.HIGHEST)
        return numerator / denominator
    attended = lax.map(one_head, (query_heads, key_heads, value_heads))
    attended = attended.transpose(1, 0, 2).reshape(QW, HEADS * HDIM)
    root_mean = jnp.sqrt(lax.optimization_barrier(jnp.mean(attended * attended, axis=1, keepdims=True)) + 1e-06)
    return (attended / root_mean * gain).astype(jnp.bfloat16)
```

```python
import math

import jax
import jax.numpy as jnp
from jax import lax
from jax.experimental import pallas as pl
from jax.experimental.pallas import tpu as pltpu
from jax.sharding import PartitionSpec as P

HDIM = 128
EXP2_SCALE = math.log2(math.e) / math.sqrt(HDIM)
VMEM_SPEC = pl.BlockSpec(memory_space=pltpu.VMEM)


def head_columns(head):
    return pl.ds(pl.multiple_of(head * HDIM, HDIM), HDIM)


def attend_kernel(query_ref, key_ref, value_ref, keep_ref, send_ref):
    rows, width = query_ref.shape
    half = rows // 2
    heads = width // HDIM
    lane = lax.broadcasted_iota(jnp.int32, (rows, HDIM), 1)

    def one_head(head, carry):
        maxima, denominators = carry
        columns = head_columns(head)
        dots = lax.dot_general(
            query_ref[:, columns],
            key_ref[:, columns],
            (((1,), (1,)), ((), ())),
            preferred_element_type=jnp.float32,
        )
        peak = jnp.max(dots, axis=1, keepdims=True)
        weights = jnp.exp2((dots - peak) * EXP2_SCALE)
        total = jnp.sum(weights, axis=1, keepdims=True)
        coarse = weights.astype(jnp.bfloat16)
        fine = (weights - coarse.astype(jnp.float32)).astype(jnp.bfloat16)
        sums = jnp.dot(
            jnp.concatenate([coarse, fine], axis=0),
            value_ref[:, columns],
            preferred_element_type=jnp.float32,
        )
        numerator = sums[:rows] + sums[rows:]
        keep_ref[:, columns] = numerator[:half]
        send_ref[:, columns] = numerator[half:]
        return jnp.where(lane == head, peak, maxima), jnp.where(lane == head, total, denominators)

    zeros = jnp.zeros((rows, HDIM), jnp.float32)
    maxima, denominators = lax.fori_loop(0, heads, one_head, (zeros, zeros), unroll=4)
    for ref, first in ((keep_ref, 0), (send_ref, half)):
        ref[:, width : width + HDIM] = maxima[first : first + half]
        ref[:, width + HDIM :] = denominators[first : first + half]


def merged_scales(here, there, width):
    max_here, max_there = here[:, width : width + HDIM], there[:, width : width + HDIM]
    maxima = jnp.maximum(max_here, max_there)
    scale_here = jnp.exp2((max_here - maxima) * EXP2_SCALE)
    scale_there = jnp.exp2((max_there - maxima) * EXP2_SCALE)
    denominators = scale_here * here[:, width + HDIM :] + scale_there * there[:, width + HDIM :]
    return maxima, denominators, scale_here, scale_there


def merge_kernel(here_ref, there_ref, keep_ref, send_ref):
    rows, padded = here_ref.shape
    width = padded - 2 * HDIM
    half = rows // 2
    maxima, denominators, scale_here, scale_there = merged_scales(here_ref, there_ref, width)
    for head in range(width // HDIM):
        columns = slice(head * HDIM, (head + 1) * HDIM)
        lane = slice(head, head + 1)
        merged = scale_here[:, lane] * here_ref[:, columns] + scale_there[:, lane] * there_ref[:, columns]
        keep_ref[:, columns] = merged[:half]
        send_ref[:, columns] = merged[half:]
    for ref, first in ((keep_ref, 0), (send_ref, half)):
        ref[:, width : width + HDIM] = maxima[first : first + half]
        ref[:, width + HDIM :] = denominators[first : first + half]


def finish_kernel(here_ref, there_ref, gain_ref, out_ref):
    rows, width = out_ref.shape
    _, denominators, scale_here, scale_there = merged_scales(here_ref, there_ref, width)
    scale_here = scale_here / denominators
    scale_there = scale_there / denominators
    squares = jnp.zeros((rows, HDIM), jnp.float32)
    attended = []
    for head in range(width // HDIM):
        columns = slice(head * HDIM, (head + 1) * HDIM)
        lane = slice(head, head + 1)
        block = scale_here[:, lane] * here_ref[:, columns] + scale_there[:, lane] * there_ref[:, columns]
        squares = squares + block * block
        attended.append(block)
    mean = jnp.sum(squares, axis=1, keepdims=True) / width
    inverse = 1.0 / jnp.sqrt(mean + 1e-06)
    for head, block in enumerate(attended):
        columns = slice(head * HDIM, (head + 1) * HDIM)
        out_ref[:, columns] = (block * inverse * gain_ref[:, columns]).astype(out_ref.dtype)


def call(kernel, out_shape, operands, flops=0, name=None):
    outs = out_shape if isinstance(out_shape, (tuple, list)) else [out_shape]
    size = sum(math.prod(a.shape) * a.dtype.itemsize for a in (*operands, *outs))
    return pl.pallas_call(
        kernel,
        out_shape=out_shape,
        in_specs=[VMEM_SPEC] * len(operands),
        out_specs=jax.tree.map(lambda _: VMEM_SPEC, out_shape),
        cost_estimate=pl.CostEstimate(flops=flops, bytes_accessed=size, transcendentals=0),
        compiler_params=pltpu.CompilerParams(vmem_limit_bytes=12 << 20),
        name=name,
    )(*operands)


def exchange(array, mask, size):
    return lax.ppermute(array, "seq", [(i, i ^ mask) for i in range(size)])


def shards(queries, keys, values, gain):
    peers = lax.axis_size("seq")
    masks = [1 << bit for bit in range(peers.bit_length() - 1)]
    rows, width = queries.shape
    window = queries
    for mask in reversed(masks):
        window = jnp.concatenate([window, exchange(window, mask, peers)], axis=0)

    def pair(count):
        return (jax.ShapeDtypeStruct((count, width + 2 * HDIM), jnp.float32),) * 2

    flops = 4 * window.shape[0] * keys.shape[0] * width
    keep, send = call(attend_kernel, pair(window.shape[0] // 2), (window, keys, values), flops, "attend")
    for mask in masks[:-1]:
        arrived = exchange(send, mask, peers)
        keep, send = call(merge_kernel, pair(keep.shape[0] // 2), (keep, arrived), 0, "merge")
    arrived = exchange(send, masks[-1], peers)
    out = jax.ShapeDtypeStruct((rows, width), jnp.bfloat16)
    return call(finish_kernel, out, (keep, arrived, gain.reshape(1, width)), 0, "finish")


def solution(mesh):
    spec = P(("grp", "seq"), None)
    return jax.shard_map(shards, mesh=mesh, in_specs=(spec, spec, spec, P()), out_specs=spec, check_vma=False)
```

```python
import math

import jax
import jax.numpy as jnp
from jax import lax
from jax.experimental import pallas as pl
from jax.experimental.pallas import tpu as pltpu
from jax.sharding import PartitionSpec as P

HDIM = 128
EXP2_SCALE = math.log2(math.e) / math.sqrt(HDIM)
FETCH_FLOPS = 6_000_000_000
VMEM_SPEC = pl.BlockSpec(memory_space=pltpu.VMEM)


def head_columns(head):
    return pl.ds(pl.multiple_of(head * HDIM, HDIM), HDIM)


def join_kernel(here_ref, there_ref, out_ref):
    out_ref[...] = jnp.concatenate([here_ref[...], there_ref[...]], axis=0)


def attend_kernel(query_here_ref, query_there_ref, key_ref, value_ref, keep_ref, send_ref, dots_ref, weights_ref):
    half, width = query_here_ref.shape
    rows = 2 * half
    heads = width // HDIM
    slots = dots_ref.shape[0]

    def score(head):
        columns = slice(head * HDIM, (head + 1) * HDIM)
        dots_ref[head % slots] = lax.dot_general(
            jnp.concatenate([query_here_ref[:, columns], query_there_ref[:, columns]], axis=0),
            key_ref[:, columns],
            (((1,), (1,)), ((), ())),
            preferred_element_type=jnp.float32,
        )

    def weigh(head):
        dots = dots_ref[head % slots]
        peak = jnp.max(dots, axis=1, keepdims=True)
        weights = jnp.exp2((dots - peak) * EXP2_SCALE)
        total = jnp.sum(weights, axis=1, keepdims=True)
        coarse = weights.astype(jnp.bfloat16)
        weights_ref[head % slots, :rows] = coarse
        weights_ref[head % slots, rows:] = (weights - coarse.astype(jnp.float32)).astype(jnp.bfloat16)
        for ref, first in ((keep_ref, 0), (send_ref, half)):
            ref[:, width + head : width + head + 1] = peak[first : first + half]
            ref[:, width + HDIM + head : width + HDIM + head + 1] = total[first : first + half]

    def accumulate(head):
        columns = slice(head * HDIM, (head + 1) * HDIM)
        sums = jnp.dot(weights_ref[head % slots], value_ref[:, columns], preferred_element_type=jnp.float32)
        numerator = sums[:rows] + sums[rows:]
        keep_ref[:, columns] = numerator[:half]
        send_ref[:, columns] = numerator[half:]

    group = slots // 2
    for ref in (keep_ref, send_ref):
        ref[:, width:] = jnp.zeros((half, 2 * HDIM), jnp.float32)
    steps = heads // group
    for step in range(steps + 2):
        for member in range(group):
            for stage, lag in ((score, 0), (weigh, 1), (accumulate, 2)):
                if 0 <= step - lag < steps:
                    stage((step - lag) * group + member)


def merged_scales(here, there, width):
    max_here, max_there = here[:, width : width + HDIM], there[:, width : width + HDIM]
    maxima = jnp.maximum(max_here, max_there)
    scale_here = jnp.exp2((max_here - maxima) * EXP2_SCALE)
    scale_there = jnp.exp2((max_there - maxima) * EXP2_SCALE)
    denominators = scale_here * here[:, width + HDIM :] + scale_there * there[:, width + HDIM :]
    return maxima, denominators, scale_here, scale_there


def merge_kernel(here_ref, there_ref, keep_ref, send_ref):
    rows, padded = here_ref.shape
    width = padded - 2 * HDIM
    half = rows // 2
    maxima, denominators, scale_here, scale_there = merged_scales(here_ref, there_ref, width)
    for head in range(width // HDIM):
        columns = slice(head * HDIM, (head + 1) * HDIM)
        lane = slice(head, head + 1)
        merged = scale_here[:, lane] * here_ref[:, columns] + scale_there[:, lane] * there_ref[:, columns]
        keep_ref[:, columns] = merged[:half]
        send_ref[:, columns] = merged[half:]
    for ref, first in ((keep_ref, 0), (send_ref, half)):
        ref[:, width : width + HDIM] = maxima[first : first + half]
        ref[:, width + HDIM :] = denominators[first : first + half]


def finish_kernel(here_ref, there_ref, gain_ref, out_ref):
    rows, width = out_ref.shape
    _, denominators, scale_here, scale_there = merged_scales(here_ref, there_ref, width)
    scale_here = scale_here / denominators
    scale_there = scale_there / denominators
    squares = jnp.zeros((rows, HDIM), jnp.float32)
    attended = []
    for head in range(width // HDIM):
        columns = slice(head * HDIM, (head + 1) * HDIM)
        lane = slice(head, head + 1)
        block = scale_here[:, lane] * here_ref[:, columns] + scale_there[:, lane] * there_ref[:, columns]
        squares = squares + block * block
        attended.append(block)
    mean = jnp.sum(squares, axis=1, keepdims=True) / width
    inverse = 1.0 / jnp.sqrt(mean + 1e-06)
    for head, block in enumerate(attended):
        columns = slice(head * HDIM, (head + 1) * HDIM)
        out_ref[:, columns] = (block * inverse * gain_ref[:, columns]).astype(out_ref.dtype)


def call(kernel, out_shape, operands, flops=0, name=None, scratch=(), limit=4 << 20):
    outs = out_shape if isinstance(out_shape, (tuple, list)) else [out_shape]
    size = sum(math.prod(a.shape) * a.dtype.itemsize for a in (*operands, *outs))
    return pl.pallas_call(
        kernel,
        out_shape=out_shape,
        in_specs=[VMEM_SPEC] * len(operands),
        out_specs=jax.tree.map(lambda _: VMEM_SPEC, out_shape),
        scratch_shapes=scratch,
        cost_estimate=pl.CostEstimate(flops=flops, bytes_accessed=size, transcendentals=0),
        compiler_params=pltpu.CompilerParams(vmem_limit_bytes=limit),
        name=name,
    )(*operands)


def exchange(array, mask, size):
    return lax.ppermute(array, "seq", [(i, i ^ mask) for i in range(size)])


def shards(queries, keys, values, gain):
    peers = lax.axis_size("seq")
    masks = [1 << bit for bit in range(peers.bit_length() - 1)]
    rows, width = queries.shape
    tokens = keys.shape[0]
    window, arrived = queries, None
    for mask in reversed(masks):
        if arrived is not None:
            both = jax.ShapeDtypeStruct((2 * window.shape[0], width), window.dtype)
            window = call(join_kernel, both, (window, arrived), FETCH_FLOPS, "join")
        arrived = exchange(window, mask, peers)
    count = 2 * window.shape[0]

    def pair(count):
        return (jax.ShapeDtypeStruct((count, width + 2 * HDIM), jnp.float32),) * 2

    keep, send = call(
        attend_kernel,
        pair(count // 2),
        (window, arrived, keys, values),
        4 * count * tokens * width,
        "attend",
        [pltpu.VMEM((4, count, tokens), jnp.float32), pltpu.VMEM((4, 2 * count, tokens), jnp.bfloat16)],
        16 << 20,
    )
    for mask in masks[:-1]:
        arrived = exchange(send, mask, peers)
        keep, send = call(merge_kernel, pair(keep.shape[0] // 2), (keep, arrived), 0, "merge")
    arrived = exchange(send, masks[-1], peers)
    out = jax.ShapeDtypeStruct((rows, width), jnp.bfloat16)
    return call(finish_kernel, out, (keep, arrived, gain.reshape(1, width)), 0, "finish")


def solution(mesh):
    spec = P(("grp", "seq"), None)
    return jax.shard_map(shards, mesh=mesh, in_specs=(spec, spec, spec, P()), out_specs=spec, check_vma=False)
```

```python
import functools
import math

import jax
import jax.numpy as jnp
from jax import lax
from jax.experimental import pallas as pl
from jax.experimental.pallas import tpu as pltpu
from jax.sharding import PartitionSpec as P

HDIM = 128
EXP2_SCALE = math.log2(math.e) / math.sqrt(HDIM)
FETCH_FLOPS = 1_000_000_000
CODE_SPAN = 250.0
VMEM_SPEC = pl.BlockSpec(memory_space=pltpu.VMEM)


def head_columns(head):
    return pl.ds(pl.multiple_of(head * HDIM, HDIM), HDIM)


def join_kernel(*refs):
    refs[-1][...] = jnp.concatenate([ref[...] for ref in refs[:-1]], axis=0)


def attend_kernel(query_here_ref, query_there_ref, key_ref, value_ref, keep_ref, send_ref, dots_ref, weights_ref):
    half, width = query_here_ref.shape
    rows = 2 * half
    heads = width // HDIM
    slots = dots_ref.shape[0]

    def score(head):
        columns = slice(head * HDIM, (head + 1) * HDIM)
        dots_ref[head % slots] = lax.dot_general(
            jnp.concatenate([query_here_ref[:, columns], query_there_ref[:, columns]], axis=0),
            key_ref[:, columns],
            (((1,), (1,)), ((), ())),
            preferred_element_type=jnp.float32,
        )

    def weigh(head):
        dots = dots_ref[head % slots]
        peak = jnp.max(dots, axis=1, keepdims=True)
        weights = jnp.exp2((dots - peak) * EXP2_SCALE)
        total = jnp.sum(weights, axis=1, keepdims=True)
        coarse = weights.astype(jnp.bfloat16)
        weights_ref[head % slots, :rows] = coarse
        weights_ref[head % slots, rows:] = (weights - coarse.astype(jnp.float32)).astype(jnp.bfloat16)
        for ref, first in ((keep_ref, 0), (send_ref, half)):
            ref[:, width + head : width + head + 1] = peak[first : first + half]
            ref[:, width + HDIM + head : width + HDIM + head + 1] = total[first : first + half]

    def accumulate(head):
        columns = slice(head * HDIM, (head + 1) * HDIM)
        sums = jnp.dot(weights_ref[head % slots], value_ref[:, columns], preferred_element_type=jnp.float32)
        numerator = sums[:rows] + sums[rows:]
        keep_ref[:, columns] = numerator[:half]
        send_ref[:, columns] = numerator[half:]

    group = slots // 2
    for ref in (keep_ref, send_ref):
        ref[:, width:] = jnp.zeros((half, 2 * HDIM), jnp.float32)
    steps = heads // group
    for step in range(steps + 2):
        for member in range(group):
            for stage, lag in ((score, 0), (weigh, 1), (accumulate, 2)):
                if 0 <= step - lag < steps:
                    stage((step - lag) * group + member)


def pack_exact(values, heads):
    lane = lax.broadcasted_iota(jnp.int32, values.shape, 1)
    first = values.astype(jnp.bfloat16).astype(jnp.float32)
    rest = values - first
    second = rest.astype(jnp.bfloat16).astype(jnp.float32)
    third = rest - second
    tail = jnp.where(lane < 2 * heads, pltpu.roll(second, heads, 1), pltpu.roll(third, 2 * heads, 1))
    return jnp.where(lane < heads, first, tail).astype(jnp.bfloat16)


def unpack_exact(packed, heads):
    terms = packed.astype(jnp.float32)
    return terms + (pltpu.roll(terms, HDIM - heads, 1) + pltpu.roll(terms, HDIM - 2 * heads, 1))


def read_statistics(ref, width, coded):
    if not coded:
        return ref[:, width : width + HDIM], ref[:, width + HDIM :], None
    heads = width // HDIM
    maxima = unpack_exact(ref[:, width : width + HDIM], heads)
    denominators = unpack_exact(ref[:, width + HDIM : width + 2 * HDIM], heads)
    return maxima, denominators, ref[:, width + 2 * HDIM :].astype(jnp.float32) * (1.0 / CODE_SPAN)


def read_numerator(ref, columns, coded):
    if not coded:
        return ref[:, columns]
    code = ref[:, columns].astype(jnp.float32)
    size = jnp.log2(jnp.abs(code)) + CODE_SPAN / 2
    return jnp.where(code < 0, -size, size)


def combine(refs, coded, width):
    statistics = [read_statistics(ref, width, c) for ref, c in zip(refs, coded)]
    maxima = functools.reduce(jnp.maximum, [m for m, _, _ in statistics])
    scales = [jnp.exp2((m - maxima) * EXP2_SCALE) for m, _, _ in statistics]
    denominators = sum(scale * d for scale, (_, d, _) in zip(scales, statistics))
    factors = [scale if unit is None else scale * unit for scale, (_, _, unit) in zip(scales, statistics)]
    return maxima, denominators, factors


def combined_numerator(refs, coded, factors, head):
    columns = slice(head * HDIM, (head + 1) * HDIM)
    lane = slice(head, head + 1)
    return sum(f[:, lane] * read_numerator(ref, columns, c) for ref, c, f in zip(refs, coded, factors))


def merge_kernel(*refs, coded):
    sources, keep_ref, send_refs = refs[: len(coded)], refs[len(coded)], refs[len(coded) + 1 :]
    block, padded = keep_ref.shape
    width = padded - 2 * HDIM
    heads = width // HDIM
    maxima, denominators, factors = combine(sources, coded, width)
    lane = lax.broadcasted_iota(jnp.int32, maxima.shape, 1)
    units = jnp.ones_like(maxima)
    for head in range(heads):
        columns = slice(head * HDIM, (head + 1) * HDIM)
        merged = combined_numerator(sources, coded, factors, head)
        keep_ref[:, columns] = merged[:block]
        largest = jnp.maximum(jnp.max(jnp.abs(merged), axis=1, keepdims=True), 1e-30)
        unit = (largest * 1.01).astype(jnp.bfloat16).astype(jnp.float32)
        size = jnp.exp2(jnp.abs(merged) * (CODE_SPAN / unit) - CODE_SPAN / 2)
        code = jnp.where(merged < 0, -size, size)
        units = jnp.where(lane == head, unit, units)
        for index, ref in enumerate(send_refs):
            ref[:, columns] = code[(index + 1) * block : (index + 2) * block].astype(jnp.bfloat16)
    keep_ref[:, width : width + HDIM] = maxima[:block]
    keep_ref[:, width + HDIM :] = denominators[:block]
    packed = [pack_exact(maxima, heads), pack_exact(denominators, heads), units.astype(jnp.bfloat16)]
    for index, ref in enumerate(send_refs):
        for place, array in enumerate(packed):
            first = width + place * HDIM
            ref[:, first : first + HDIM] = array[(index + 1) * block : (index + 2) * block]


def finish_kernel(*refs, coded):
    sources, gain_ref, out_ref = refs[: len(coded)], refs[-2], refs[-1]
    rows, width = out_ref.shape
    _, denominators, factors = combine(sources, coded, width)
    factors = [factor / denominators for factor in factors]
    squares = jnp.zeros((rows, HDIM), jnp.float32)
    attended = []
    for head in range(width // HDIM):
        block = combined_numerator(sources, coded, factors, head)
        squares = squares + block * block
        attended.append(block)
    mean = jnp.sum(squares, axis=1, keepdims=True) / width
    inverse = 1.0 / jnp.sqrt(mean + 1e-06)
    for head, block in enumerate(attended):
        columns = slice(head * HDIM, (head + 1) * HDIM)
        out_ref[:, columns] = (block * inverse * gain_ref[:, columns]).astype(out_ref.dtype)


def call(kernel, out_shape, operands, flops=0, name=None, scratch=(), limit=4 << 20):
    outs = out_shape if isinstance(out_shape, (tuple, list)) else [out_shape]
    size = sum(math.prod(a.shape) * a.dtype.itemsize for a in (*operands, *outs))
    return pl.pallas_call(
        kernel,
        out_shape=out_shape,
        in_specs=[VMEM_SPEC] * len(operands),
        out_specs=jax.tree.map(lambda _: VMEM_SPEC, out_shape),
        scratch_shapes=scratch,
        cost_estimate=pl.CostEstimate(flops=flops, bytes_accessed=size, transcendentals=0),
        compiler_params=pltpu.CompilerParams(vmem_limit_bytes=limit),
        name=name,
    )(*operands)


def exchange(array, mask, size):
    return lax.ppermute(array, "seq", [(i, i ^ mask) for i in range(size)])


def mask_groups(peers):
    bits = [1 << bit for bit in range(peers.bit_length() - 1)]
    cores, chips = bits[:1], bits[1:]
    groups = [chips[first : first + 3] for first in range(0, len(chips), 3)]
    return [[sum(b for i, b in enumerate(g) if j >> i & 1) for j in range(1, 1 << len(g))] for g in (*groups[::-1], cores)]


def join(pieces):
    while len(pieces) > 1:
        step = 2 if len(pieces) > 4 else len(pieces)
        joined = []
        for first in range(0, len(pieces), step):
            part = pieces[first : first + step]
            shape = (sum(p.shape[0] for p in part), part[0].shape[1])
            joined.append(call(join_kernel, jax.ShapeDtypeStruct(shape, part[0].dtype), part, FETCH_FLOPS, "join"))
        pieces = joined
    return pieces[0]


def shards(queries, keys, values, gain):
    peers = lax.axis_size("seq")
    groups = mask_groups(peers)
    rows, width = queries.shape
    tokens = keys.shape[0]
    window = queries
    for masks in groups[:-1]:
        window = join([window, *(exchange(window, mask, peers) for mask in masks)])
    arrived = exchange(window, groups[-1][0], peers)
    half = window.shape[0]

    plain = lambda count: jax.ShapeDtypeStruct((count, width + 2 * HDIM), jnp.float32)
    code = lambda count: jax.ShapeDtypeStruct((count, width + 3 * HDIM), jnp.bfloat16)
    keep, send = call(
        attend_kernel,
        (plain(half), plain(half)),
        (window, arrived, keys, values),
        8 * half * tokens * width,
        "attend",
        [pltpu.VMEM((4, 2 * half, tokens), jnp.float32), pltpu.VMEM((4, 4 * half, tokens), jnp.bfloat16)],
        16 << 20,
    )
    sources, coded = [keep, exchange(send, groups[-1][0], peers)], (False, False)
    for masks in groups[-2::-1]:
        count = sources[0].shape[0] // (len(masks) + 1)
        shapes = (plain(count), *[code(count)] * len(masks))
        keep, *sends = call(functools.partial(merge_kernel, coded=coded), shapes, sources, 0, "merge")
        sources = [keep, *(exchange(part, mask, peers) for part, mask in zip(sends, masks))]
        coded = (False, *[True] * len(masks))
    out = jax.ShapeDtypeStruct((rows, width), jnp.bfloat16)
    return call(functools.partial(finish_kernel, coded=coded), out, (*sources, gain.reshape(1, width)), 0, "finish")


def solution(mesh):
    spec = P(("grp", "seq"), None)
    return jax.shard_map(shards, mesh=mesh, in_specs=(spec, spec, spec, P()), out_specs=spec, check_vma=False)
```

```python
import functools
import math

import jax
import jax.numpy as jnp
from jax import lax
from jax.experimental import pallas as pl
from jax.experimental.pallas import tpu as pltpu
from jax.sharding import PartitionSpec as P

HDIM = 128
EXP2_SCALE = math.log2(math.e) / math.sqrt(HDIM)
FETCH_FLOPS = 1_500_000_000
CODE_SPAN = 250.0
VMEM_SPEC = pl.BlockSpec(memory_space=pltpu.VMEM)


def copy_kernel(source_ref, out_ref):
    out_ref[...] = source_ref[...]


def join_kernel(here_ref, there_ref, out_ref):
    out_ref[...] = jnp.concatenate([here_ref[...], there_ref[...]], axis=0)


def attend_kernel(query_here_ref, query_there_ref, key_ref, value_ref, keep_ref, send_ref, dots_ref, weights_ref):
    half, width = query_here_ref.shape
    rows = 2 * half
    heads = width // HDIM
    slots = dots_ref.shape[0]

    def score(head):
        columns = slice(head * HDIM, (head + 1) * HDIM)
        dots_ref[head % slots] = lax.dot_general(
            jnp.concatenate([query_here_ref[:, columns], query_there_ref[:, columns]], axis=0),
            key_ref[:, columns],
            (((1,), (1,)), ((), ())),
            preferred_element_type=jnp.float32,
        )

    def weigh(head):
        dots = dots_ref[head % slots]
        peak = jnp.max(dots, axis=1, keepdims=True)
        weights = jnp.exp2((dots - peak) * EXP2_SCALE)
        total = jnp.sum(weights, axis=1, keepdims=True)
        coarse = weights.astype(jnp.bfloat16)
        weights_ref[head % slots, :rows] = coarse
        weights_ref[head % slots, rows:] = (weights - coarse.astype(jnp.float32)).astype(jnp.bfloat16)
        for ref, first in ((keep_ref, 0), (send_ref, half)):
            ref[:, width + head : width + head + 1] = peak[first : first + half]
            ref[:, width + HDIM + head : width + HDIM + head + 1] = total[first : first + half]

    def accumulate(head):
        columns = slice(head * HDIM, (head + 1) * HDIM)
        sums = jnp.dot(weights_ref[head % slots], value_ref[:, columns], preferred_element_type=jnp.float32)
        numerator = sums[:rows] + sums[rows:]
        keep_ref[:, columns] = numerator[:half]
        send_ref[:, columns] = numerator[half:]

    group = slots // 2
    for ref in (keep_ref, send_ref):
        ref[:, width:] = jnp.zeros((half, 2 * HDIM), jnp.float32)
    steps = heads // group
    for step in range(steps + 2):
        for member in range(group):
            for stage, lag in ((score, 0), (weigh, 1), (accumulate, 2)):
                if 0 <= step - lag < steps:
                    stage((step - lag) * group + member)


def pack_exact(values, heads):
    lane = lax.broadcasted_iota(jnp.int32, values.shape, 1)
    first = values.astype(jnp.bfloat16).astype(jnp.float32)
    rest = values - first
    second = rest.astype(jnp.bfloat16).astype(jnp.float32)
    third = rest - second
    tail = jnp.where(lane < 2 * heads, pltpu.roll(second, heads, 1), pltpu.roll(third, 2 * heads, 1))
    return jnp.where(lane < heads, first, tail).astype(jnp.bfloat16)


def unpack_exact(packed, heads):
    terms = packed.astype(jnp.float32)
    return terms + (pltpu.roll(terms, HDIM - heads, 1) + pltpu.roll(terms, HDIM - 2 * heads, 1))


def read_statistics(ref, width, coded):
    if not coded:
        return ref[:, width : width + HDIM], ref[:, width + HDIM :], None
    heads = width // HDIM
    maxima = unpack_exact(ref[:, width : width + HDIM], heads)
    denominators = unpack_exact(ref[:, width + HDIM : width + 2 * HDIM], heads)
    return maxima, denominators, ref[:, width + 2 * HDIM :].astype(jnp.float32) * (1.0 / CODE_SPAN)


def read_numerator(ref, columns, coded):
    if not coded:
        return ref[:, columns]
    code = ref[:, columns].astype(jnp.float32)
    size = jnp.log2(jnp.abs(code)) + CODE_SPAN / 2
    return jnp.where(code < 0, -size, size)


def combine(refs, coded, width):
    statistics = [read_statistics(ref, width, c) for ref, c in zip(refs, coded)]
    maxima = functools.reduce(jnp.maximum, [m for m, _, _ in statistics])
    scales = [jnp.exp2((m - maxima) * EXP2_SCALE) for m, _, _ in statistics]
    denominators = sum(scale * d for scale, (_, d, _) in zip(scales, statistics))
    factors = [scale if unit is None else scale * unit for scale, (_, _, unit) in zip(scales, statistics)]
    return maxima, denominators, factors


def combined_numerator(refs, coded, factors, head):
    columns = slice(head * HDIM, (head + 1) * HDIM)
    lane = slice(head, head + 1)
    return sum(f[:, lane] * read_numerator(ref, columns, c) for ref, c, f in zip(refs, coded, factors))


def merge_kernel(here_ref, there_ref, keep_ref, send_ref, *, coded):
    sources = (here_ref, there_ref)
    half, padded = keep_ref.shape
    width = padded - 2 * HDIM
    heads = width // HDIM
    maxima, denominators, factors = combine(sources, coded, width)
    lane = lax.broadcasted_iota(jnp.int32, (half, HDIM), 1)
    units = jnp.ones((half, HDIM), jnp.float32)
    for head in range(heads):
        columns = slice(head * HDIM, (head + 1) * HDIM)
        merged = combined_numerator(sources, coded, factors, head)
        keep_ref[:, columns] = merged[:half]
        merged = merged[half:]
        size = jnp.abs(merged)
        largest = jnp.maximum(jnp.max(size, axis=1, keepdims=True), 1e-30)
        unit = (largest * 1.01).astype(jnp.bfloat16).astype(jnp.float32)
        code = jnp.exp2(size * (CODE_SPAN / unit) - CODE_SPAN / 2)
        send_ref[:, columns] = jnp.where(merged < 0, -code, code).astype(jnp.bfloat16)
        units = jnp.where(lane == head, unit, units)
    keep_ref[:, width : width + HDIM] = maxima[:half]
    keep_ref[:, width + HDIM :] = denominators[:half]
    send_ref[:, width : width + HDIM] = pack_exact(maxima[half:], heads)
    send_ref[:, width + HDIM : width + 2 * HDIM] = pack_exact(denominators[half:], heads)
    send_ref[:, width + 2 * HDIM :] = units.astype(jnp.bfloat16)


def finish_kernel(here_ref, there_ref, gain_ref, out_ref, *, coded):
    sources = (here_ref, there_ref)
    rows, width = out_ref.shape
    _, denominators, factors = combine(sources, coded, width)
    factors = [factor / denominators for factor in factors]
    squares = jnp.zeros((rows, HDIM), jnp.float32)
    attended = []
    for head in range(width // HDIM):
        block = combined_numerator(sources, coded, factors, head)
        squares = squares + block * block
        attended.append(block)
    mean = jnp.sum(squares, axis=1, keepdims=True) / width
    inverse = 1.0 / jnp.sqrt(mean + 1e-06)
    for head, block in enumerate(attended):
        columns = slice(head * HDIM, (head + 1) * HDIM)
        out_ref[:, columns] = (block * inverse * gain_ref[:, columns]).astype(out_ref.dtype)


def call(kernel, out_shape, operands, flops=0, scratch=(), limit=4 << 20):
    outs = out_shape if isinstance(out_shape, (tuple, list)) else [out_shape]
    size = sum(math.prod(a.shape) * a.dtype.itemsize for a in (*operands, *outs))
    return pl.pallas_call(
        kernel,
        out_shape=out_shape,
        in_specs=[VMEM_SPEC] * len(operands),
        out_specs=jax.tree.map(lambda _: VMEM_SPEC, out_shape),
        scratch_shapes=scratch,
        cost_estimate=pl.CostEstimate(flops=flops, bytes_accessed=size, transcendentals=0),
        compiler_params=pltpu.CompilerParams(vmem_limit_bytes=limit),
    )(*operands)


def exchange(array, masks):
    return lax.ppermute(array, "seq", [(i, i ^ masks[i % 2]) for i in range(lax.axis_size("seq"))])


def chip_stages(peers):
    first = [1 << bit for bit in range(1, peers.bit_length() - 1)]
    second = [*first[1::-1], *first[2:]]
    return list(zip(first, second))


def shards(queries, keys, values, gain):
    stages = chip_stages(lax.axis_size("seq"))
    cores = (1, 1)
    rows, width = queries.shape
    tokens = keys.shape[0]
    gain = call(copy_kernel, jax.ShapeDtypeStruct((1, width), gain.dtype), [gain.reshape(1, width)], FETCH_FLOPS)
    window = queries
    for masks in reversed(stages):
        arrived = exchange(window, masks)
        both = jax.ShapeDtypeStruct((2 * window.shape[0], width), window.dtype)
        window = call(join_kernel, both, [window, arrived], FETCH_FLOPS)
    arrived = exchange(window, cores)
    half = window.shape[0]

    plain = lambda count: jax.ShapeDtypeStruct((count, width + 2 * HDIM), jnp.float32)
    code = lambda count: jax.ShapeDtypeStruct((count, width + 3 * HDIM), jnp.bfloat16)
    keep, send = call(
        attend_kernel,
        (plain(half), plain(half)),
        (window, arrived, keys, values),
        8 * half * tokens * width,
        [pltpu.VMEM((4, 2 * half, tokens), jnp.float32), pltpu.VMEM((4, 4 * half, tokens), jnp.bfloat16)],
        16 << 20,
    )
    sources, coded = (keep, exchange(send, cores)), (False, False)
    for masks in stages:
        half = half // 2
        kernel = functools.partial(merge_kernel, coded=coded)
        keep, send = call(kernel, (plain(half), code(half)), sources, 0)
        sources, coded = (keep, exchange(send, masks)), (False, True)
    out = jax.ShapeDtypeStruct((rows, width), jnp.bfloat16)
    return call(functools.partial(finish_kernel, coded=coded), out, (*sources, gain), 0)


def solution(mesh):
    spec = P(("grp", "seq"), None)
    return jax.shard_map(shards, mesh=mesh, in_specs=(spec, spec, spec, P()), out_specs=spec, check_vma=False)
```

```python
import functools
import math

import jax
import jax.numpy as jnp
from jax import lax
from jax.experimental import pallas as pl
from jax.experimental.pallas import tpu as pltpu
from jax.sharding import PartitionSpec as P

HDIM = 128
EXP2_SCALE = math.log2(math.e) / math.sqrt(HDIM)
FETCH_FLOPS = 1_500_000_000
CHAINS = 2
CODE_SPAN = 250.0
VMEM_SPEC = pl.BlockSpec(memory_space=pltpu.VMEM)


def copy_kernel(source_ref, out_ref):
    out_ref[...] = source_ref[...]


def join_kernel(here_ref, there_ref, *out_refs):
    for index, ref in enumerate(out_refs):
        width = ref.shape[1]
        columns = slice(index * width, (index + 1) * width)
        ref[...] = jnp.concatenate([here_ref[:, columns], there_ref[:, columns]], axis=0)


def attend_kernel(
    query_here_ref, query_there_ref, key_ref, value_ref, keep_ref, send_ref, dots_ref, weights_ref, *, first_head
):
    half, width = query_here_ref.shape
    rows = 2 * half
    heads = width // HDIM
    slots = dots_ref.shape[0]

    def shifted(head):
        return slice((first_head + head) * HDIM, (first_head + head + 1) * HDIM)

    def score(head):
        columns = slice(head * HDIM, (head + 1) * HDIM)
        dots_ref[head % slots] = lax.dot_general(
            jnp.concatenate([query_here_ref[:, columns], query_there_ref[:, columns]], axis=0),
            key_ref[:, shifted(head)],
            (((1,), (1,)), ((), ())),
            preferred_element_type=jnp.float32,
        )

    def weigh(head):
        dots = dots_ref[head % slots]
        peak = jnp.max(dots, axis=1, keepdims=True)
        weights = jnp.exp2((dots - peak) * EXP2_SCALE)
        total = jnp.sum(weights, axis=1, keepdims=True)
        coarse = weights.astype(jnp.bfloat16)
        weights_ref[head % slots, :rows] = coarse
        weights_ref[head % slots, rows:] = (weights - coarse.astype(jnp.float32)).astype(jnp.bfloat16)
        for ref, first in ((keep_ref, 0), (send_ref, half)):
            ref[:, width + head : width + head + 1] = peak[first : first + half]
            ref[:, width + HDIM + head : width + HDIM + head + 1] = total[first : first + half]

    def accumulate(head):
        columns = slice(head * HDIM, (head + 1) * HDIM)
        sums = jnp.dot(weights_ref[head % slots], value_ref[:, shifted(head)], preferred_element_type=jnp.float32)
        numerator = sums[:rows] + sums[rows:]
        keep_ref[:, columns] = numerator[:half]
        send_ref[:, columns] = numerator[half:]

    group = slots // 2
    for ref in (keep_ref, send_ref):
        ref[:, width:] = jnp.zeros((half, 2 * HDIM), jnp.float32)
    steps = heads // group
    for step in range(steps + 2):
        for member in range(group):
            for stage, lag in ((score, 0), (weigh, 1), (accumulate, 2)):
                if 0 <= step - lag < steps:
                    stage((step - lag) * group + member)


def pack_exact(values, heads):
    lane = lax.broadcasted_iota(jnp.int32, values.shape, 1)
    first = values.astype(jnp.bfloat16).astype(jnp.float32)
    rest = values - first
    second = rest.astype(jnp.bfloat16).astype(jnp.float32)
    third = rest - second
    tail = jnp.where(lane < 2 * heads, pltpu.roll(second, heads, 1), pltpu.roll(third, 2 * heads, 1))
    return jnp.where(lane < heads, first, tail).astype(jnp.bfloat16)


def unpack_exact(packed, heads):
    terms = packed.astype(jnp.float32)
    return terms + (pltpu.roll(terms, HDIM - heads, 1) + pltpu.roll(terms, HDIM - 2 * heads, 1))


def read_statistics(ref, width, coded):
    if not coded:
        return ref[:, width : width + HDIM], ref[:, width + HDIM :], None
    heads = width // HDIM
    maxima = unpack_exact(ref[:, width : width + HDIM], heads)
    denominators = unpack_exact(ref[:, width + HDIM : width + 2 * HDIM], heads)
    return maxima, denominators, ref[:, width + 2 * HDIM :].astype(jnp.float32) * (1.0 / CODE_SPAN)


def read_numerator(ref, columns, coded):
    if not coded:
        return ref[:, columns]
    code = ref[:, columns].astype(jnp.float32)
    size = jnp.log2(jnp.abs(code)) + CODE_SPAN / 2
    return jnp.where(code < 0, -size, size)


def combine(refs, coded, width):
    statistics = [read_statistics(ref, width, kind == "coded") for ref, kind in zip(refs, coded)]
    maxima = functools.reduce(jnp.maximum, [m for m, _, _ in statistics])
    scales = [jnp.exp2((m - maxima) * EXP2_SCALE) for m, _, _ in statistics]
    denominators = sum(scale * d for scale, (_, d, _) in zip(scales, statistics))
    inverse = 1.0 / denominators
    factors = []
    for kind, scale, (_, d, unit) in zip(coded, scales, statistics):
        factor = scale * inverse
        if kind != "sums":
            factor = factor * d
        factors.append(factor if unit is None else factor * unit)
    return maxima, denominators, factors


def combined_mean(refs, coded, factors, head):
    columns = slice(head * HDIM, (head + 1) * HDIM)
    lane = slice(head, head + 1)
    return sum(f[:, lane] * read_numerator(ref, columns, k == "coded") for ref, k, f in zip(refs, coded, factors))


def section(ref, index, width):
    return ref.at[:, index * width : (index + 1) * width]


def merge_kernel(*refs, kinds, chains):
    all_keep_ref, all_send_ref, means_ref = refs[2 * chains :]
    half, width = means_ref.shape
    heads = width // HDIM
    lane = lax.broadcasted_iota(jnp.int32, (half, HDIM), 1)
    for chain in range(chains):
        sources = refs[2 * chain : 2 * chain + 2]
        keep_ref = section(all_keep_ref, chain, width + 2 * HDIM)
        send_ref = section(all_send_ref, chain, width + 3 * HDIM)
        maxima, denominators, factors = combine(sources, kinds, width)
        largest = jnp.ones((half, HDIM), jnp.float32)
        for head in range(heads):
            columns = slice(head * HDIM, (head + 1) * HDIM)
            merged = combined_mean(sources, kinds, factors, head)
            keep_ref[:, columns] = merged[:half]
            means_ref[:, columns] = merged[half:]
            largest = jnp.where(lane == head, jnp.max(jnp.abs(merged[half:]), axis=1, keepdims=True), largest)
        units = (jnp.maximum(largest, 1e-30) * 1.01).astype(jnp.bfloat16)
        steps = CODE_SPAN / units.astype(jnp.float32)
        for head in range(heads):
            columns = slice(head * HDIM, (head + 1) * HDIM)
            mean = means_ref[:, columns]
            code = jnp.exp2(jnp.abs(mean) * steps[:, head : head + 1] - CODE_SPAN / 2)
            send_ref[:, columns] = jnp.where(mean < 0, -code, code).astype(jnp.bfloat16)
        keep_ref[:, width : width + HDIM] = maxima[:half]
        keep_ref[:, width + HDIM :] = denominators[:half]
        send_ref[:, width : width + HDIM] = pack_exact(maxima[half:], heads)
        send_ref[:, width + HDIM : width + 2 * HDIM] = pack_exact(denominators[half:], heads)
        send_ref[:, width + 2 * HDIM :] = units


def finish_kernel(all_here_ref, all_there_ref, gain_ref, out_ref, *, kinds, chains):
    rows, all_width = out_ref.shape
    width = all_width // chains
    squares = jnp.zeros((rows, HDIM), jnp.float32)
    attended = []
    for chain in range(chains):
        sources = (section(all_here_ref, chain, width + 2 * HDIM), section(all_there_ref, chain, width + 3 * HDIM))
        _, _, factors = combine(sources, kinds, width)
        for head in range(width // HDIM):
            block = combined_mean(sources, kinds, factors, head)
            squares = squares + block * block
            attended.append(block)
    mean = jnp.sum(squares, axis=1, keepdims=True) / all_width
    inverse = 1.0 / jnp.sqrt(mean + 1e-06)
    for head, block in enumerate(attended):
        columns = slice(head * HDIM, (head + 1) * HDIM)
        out_ref[:, columns] = (block * inverse * gain_ref[:, columns]).astype(out_ref.dtype)


def call(kernel, out_shape, operands, flops=0, scratch=(), limit=4 << 20):
    outs = out_shape if isinstance(out_shape, (tuple, list)) else [out_shape]
    size = sum(math.prod(a.shape) * a.dtype.itemsize for a in (*operands, *outs))
    return pl.pallas_call(
        kernel,
        out_shape=out_shape,
        in_specs=[VMEM_SPEC] * len(operands),
        out_specs=jax.tree.map(lambda _: VMEM_SPEC, out_shape),
        scratch_shapes=scratch,
        cost_estimate=pl.CostEstimate(flops=flops, bytes_accessed=size, transcendentals=0),
        compiler_params=pltpu.CompilerParams(vmem_limit_bytes=limit),
    )(*operands)


def exchange(array, mask):
    return lax.ppermute(array, "seq", [(i, i ^ mask) for i in range(lax.axis_size("seq"))])


def shards(queries, keys, values, gain):
    masks = [1 << bit for bit in range(lax.axis_size("seq").bit_length() - 1)]
    core, chips = masks[0], masks[1:]
    rows, width = queries.shape
    part = width // CHAINS
    tokens = keys.shape[0]
    gain = call(copy_kernel, jax.ShapeDtypeStruct((1, width), gain.dtype), [gain.reshape(1, width)], FETCH_FLOPS)

    def joined(window, arrived, parts):
        shape = jax.ShapeDtypeStruct((2 * window.shape[0], window.shape[1] // parts), window.dtype)
        return call(join_kernel, (shape,) * parts, [window, arrived], FETCH_FLOPS)

    windows = joined(queries, exchange(queries, chips[-1]), CHAINS)
    for mask in chips[-2::-1]:
        arrived = [exchange(w, mask) for w in windows]
        windows = [joined(w, a, 1)[0] for w, a in zip(windows, arrived)]
    arrived = [exchange(w, core) for w in windows]
    half = windows[0].shape[0]

    plain = lambda count, parts: jax.ShapeDtypeStruct((count, parts * (part + 2 * HDIM)), jnp.float32)
    code = lambda count, parts: jax.ShapeDtypeStruct((count, parts * (part + 3 * HDIM)), jnp.bfloat16)

    def attend(chain):
        return call(
            functools.partial(attend_kernel, first_head=chain * part // HDIM),
            (plain(half, 1), plain(half, 1)),
            (windows[chain], arrived[chain], keys, values),
            8 * half * tokens * part,
            [pltpu.VMEM((4, 2 * half, tokens), jnp.float32), pltpu.VMEM((4, 4 * half, tokens), jnp.bfloat16)],
            16 << 20,
        )

    def merge(sources, kinds, count, chains):
        kernel = functools.partial(merge_kernel, kinds=kinds, chains=chains)
        shapes = (plain(count, chains), code(count, chains))
        return call(kernel, shapes, sources, 0, [pltpu.VMEM((count, part), jnp.float32)])

    parts = [attend(chain) for chain in range(CHAINS)]
    pairs = [(keep, exchange(send, core)) for keep, send in parts]
    kinds = ("sums", "sums")
    for mask in chips[:-1]:
        half = half // 2
        parts = [merge(pair, kinds, half, 1) for pair in pairs]
        pairs = [(keep, exchange(send, mask)) for keep, send in parts]
        kinds = ("means", "coded")
    keep, send = merge([array for pair in pairs for array in pair], kinds, half // 2, CHAINS)
    kernel = functools.partial(finish_kernel, kinds=("means", "coded"), chains=CHAINS)
    out = jax.ShapeDtypeStruct((rows, width), jnp.bfloat16)
    return call(kernel, out, (keep, exchange(send, chips[-1]), gain), 0)


def solution(mesh):
    spec = P(("grp", "seq"), None)
    return jax.shard_map(shards, mesh=mesh, in_specs=(spec, spec, spec, P()), out_specs=spec, check_vma=False)
```

```python
import functools
import math

import jax
import jax.numpy as jnp
from jax import lax
from jax.experimental import pallas as pl
from jax.experimental.pallas import tpu as pltpu
from jax.sharding import PartitionSpec as P

HDIM = 128
EXP2_SCALE = math.log2(math.e) / math.sqrt(HDIM)
FETCH_FLOPS = 1_500_000_000
CHAINS = 2
CODE_SPAN = 250.0
VMEM_SPEC = pl.BlockSpec(memory_space=pltpu.VMEM)


def copy_kernel(source_ref, out_ref):
    out_ref[...] = source_ref[...]


def join_kernel(here_ref, there_ref, *out_refs):
    for index, ref in enumerate(out_refs):
        width = ref.shape[1]
        columns = slice(index * width, (index + 1) * width)
        ref[...] = jnp.concatenate([here_ref[:, columns], there_ref[:, columns]], axis=0)


def attend_kernel(
    query_here_ref, query_there_ref, key_ref, value_ref, keep_ref, send_ref, dots_ref, weights_ref, *, first_head
):
    half, width = query_here_ref.shape
    rows = 2 * half
    heads = width // HDIM
    slots = dots_ref.shape[0]

    def shifted(head):
        return slice((first_head + head) * HDIM, (first_head + head + 1) * HDIM)

    def score(head):
        columns = slice(head * HDIM, (head + 1) * HDIM)
        dots_ref[head % slots] = lax.dot_general(
            jnp.concatenate([query_here_ref[:, columns], query_there_ref[:, columns]], axis=0),
            key_ref[:, shifted(head)],
            (((1,), (1,)), ((), ())),
            preferred_element_type=jnp.float32,
        )

    def weigh(head):
        dots = dots_ref[head % slots]
        peak = jnp.max(dots, axis=1, keepdims=True)
        weights = jnp.exp2((dots - peak) * EXP2_SCALE)
        total = jnp.sum(weights, axis=1, keepdims=True)
        coarse = weights.astype(jnp.bfloat16)
        weights_ref[head % slots, :rows] = coarse
        weights_ref[head % slots, rows:] = (weights - coarse.astype(jnp.float32)).astype(jnp.bfloat16)
        for ref, first in ((keep_ref, 0), (send_ref, half)):
            ref[:, width + head : width + head + 1] = peak[first : first + half]
            ref[:, width + HDIM + head : width + HDIM + head + 1] = total[first : first + half]

    def accumulate(head):
        columns = slice(head * HDIM, (head + 1) * HDIM)
        sums = jnp.dot(weights_ref[head % slots], value_ref[:, shifted(head)], preferred_element_type=jnp.float32)
        numerator = sums[:rows] + sums[rows:]
        keep_ref[:, columns] = numerator[:half]
        send_ref[:, columns] = numerator[half:]

    group = slots // 2
    for ref in (keep_ref, send_ref):
        ref[:, width:] = jnp.zeros((half, 2 * HDIM), jnp.float32)
    steps = heads // group
    for step in range(steps + 2):
        for member in range(group):
            for stage, lag in ((score, 0), (weigh, 1), (accumulate, 2)):
                if 0 <= step - lag < steps:
                    stage((step - lag) * group + member)


def pack_exact(values, heads):
    lane = lax.broadcasted_iota(jnp.int32, values.shape, 1)
    first = values.astype(jnp.bfloat16).astype(jnp.float32)
    rest = values - first
    second = rest.astype(jnp.bfloat16).astype(jnp.float32)
    third = rest - second
    tail = jnp.where(lane < 2 * heads, pltpu.roll(second, heads, 1), pltpu.roll(third, 2 * heads, 1))
    return jnp.where(lane < heads, first, tail).astype(jnp.bfloat16)


def unpack_exact(packed, heads):
    terms = packed.astype(jnp.float32)
    return terms + (pltpu.roll(terms, HDIM - heads, 1) + pltpu.roll(terms, HDIM - 2 * heads, 1))


def read_statistics(ref, width, coded):
    if not coded:
        return ref[:, width : width + HDIM], ref[:, width + HDIM :], None
    heads = width // HDIM
    maxima = unpack_exact(ref[:, width : width + HDIM], heads)
    denominators = unpack_exact(ref[:, width + HDIM : width + 2 * HDIM], heads)
    return maxima, denominators, ref[:, width + 2 * HDIM :].astype(jnp.float32) * (1.0 / CODE_SPAN)


def read_numerator(ref, columns, coded):
    if not coded:
        return ref[:, columns]
    code = ref[:, columns].astype(jnp.float32)
    size = jnp.log2(jnp.abs(code)) + CODE_SPAN / 2
    return jnp.where(code < 0, -size, size)


def combine(refs, coded, width):
    statistics = [read_statistics(ref, width, kind == "coded") for ref, kind in zip(refs, coded)]
    maxima = functools.reduce(jnp.maximum, [m for m, _, _ in statistics])
    scales = [jnp.exp2((m - maxima) * EXP2_SCALE) for m, _, _ in statistics]
    denominators = sum(scale * d for scale, (_, d, _) in zip(scales, statistics))
    inverse = 1.0 / denominators
    factors = []
    for kind, scale, (_, d, unit) in zip(coded, scales, statistics):
        factor = scale * inverse
        if kind != "sums":
            factor = factor * d
        factors.append(factor if unit is None else factor * unit)
    return maxima, denominators, factors


def combined_mean(refs, coded, factors, head):
    columns = slice(head * HDIM, (head + 1) * HDIM)
    lane = slice(head, head + 1)
    return sum(f[:, lane] * read_numerator(ref, columns, k == "coded") for ref, k, f in zip(refs, coded, factors))


def section(ref, index, width):
    return ref.at[:, index * width : (index + 1) * width]


def merge_kernel(*refs, kinds, chains):
    all_keep_ref, all_send_ref, means_ref = refs[2 * chains :]
    half, width = means_ref.shape
    heads = width // HDIM
    lane = lax.broadcasted_iota(jnp.int32, (half, HDIM), 1)
    for chain in range(chains):
        sources = refs[2 * chain : 2 * chain + 2]
        keep_ref = section(all_keep_ref, chain, width + 2 * HDIM)
        send_ref = section(all_send_ref, chain, width + 3 * HDIM)
        maxima, denominators, factors = combine(sources, kinds, width)
        largest = jnp.full((half, HDIM), 1e-30, jnp.float32)
        for head in range(heads):
            columns = slice(head * HDIM, (head + 1) * HDIM)
            merged = combined_mean(sources, kinds, factors, head)
            keep_ref[:, columns] = merged[:half]
            means_ref[:, columns] = merged[half:]
            largest = jnp.maximum(largest, jnp.abs(merged[half:]))
        units = (jnp.max(largest, axis=1, keepdims=True) * 1.01).astype(jnp.bfloat16)
        step = jnp.broadcast_to(CODE_SPAN / units.astype(jnp.float32), largest.shape)
        for head in range(heads):
            columns = slice(head * HDIM, (head + 1) * HDIM)
            mean = means_ref[:, columns]
            code = jnp.exp2(jnp.abs(mean) * step - CODE_SPAN / 2)
            send_ref[:, columns] = jnp.where(mean < 0, -code, code).astype(jnp.bfloat16)
        keep_ref[:, width : width + HDIM] = maxima[:half]
        keep_ref[:, width + HDIM :] = denominators[:half]
        send_ref[:, width : width + HDIM] = pack_exact(maxima[half:], heads)
        send_ref[:, width + HDIM : width + 2 * HDIM] = pack_exact(denominators[half:], heads)
        send_ref[:, width + 2 * HDIM :] = jnp.broadcast_to(units, largest.shape)


def finish_kernel(all_here_ref, all_there_ref, gain_ref, out_ref, *, kinds, chains):
    rows, all_width = out_ref.shape
    width = all_width // chains
    squares = jnp.zeros((rows, HDIM), jnp.float32)
    attended = []
    for chain in range(chains):
        sources = (section(all_here_ref, chain, width + 2 * HDIM), section(all_there_ref, chain, width + 3 * HDIM))
        _, _, factors = combine(sources, kinds, width)
        for head in range(width // HDIM):
            block = combined_mean(sources, kinds, factors, head)
            squares = squares + block * block
            attended.append(block)
    mean = jnp.sum(squares, axis=1, keepdims=True) / all_width
    inverse = 1.0 / jnp.sqrt(mean + 1e-06)
    for head, block in enumerate(attended):
        columns = slice(head * HDIM, (head + 1) * HDIM)
        out_ref[:, columns] = (block * inverse * gain_ref[:, columns]).astype(out_ref.dtype)


def call(kernel, out_shape, operands, flops=0, scratch=(), limit=4 << 20):
    outs = out_shape if isinstance(out_shape, (tuple, list)) else [out_shape]
    size = sum(math.prod(a.shape) * a.dtype.itemsize for a in (*operands, *outs))
    return pl.pallas_call(
        kernel,
        out_shape=out_shape,
        in_specs=[VMEM_SPEC] * len(operands),
        out_specs=jax.tree.map(lambda _: VMEM_SPEC, out_shape),
        scratch_shapes=scratch,
        cost_estimate=pl.CostEstimate(flops=flops, bytes_accessed=size, transcendentals=0),
        compiler_params=pltpu.CompilerParams(vmem_limit_bytes=limit),
    )(*operands)


def exchange(array, mask):
    return lax.ppermute(array, "seq", [(i, i ^ mask) for i in range(lax.axis_size("seq"))])


def shards(queries, keys, values, gain):
    masks = [1 << bit for bit in range(lax.axis_size("seq").bit_length() - 1)]
    core, chips = masks[0], masks[1:]
    rows, width = queries.shape
    part = width // CHAINS
    tokens = keys.shape[0]
    gain = call(copy_kernel, jax.ShapeDtypeStruct((1, width), gain.dtype), [gain.reshape(1, width)], FETCH_FLOPS)

    def joined(window, arrived, parts):
        shape = jax.ShapeDtypeStruct((2 * window.shape[0], window.shape[1] // parts), window.dtype)
        return call(join_kernel, (shape,) * parts, [window, arrived], FETCH_FLOPS)

    windows = joined(queries, exchange(queries, chips[-1]), CHAINS)
    for mask in chips[-2::-1]:
        arrived = [exchange(w, mask) for w in windows]
        windows = [joined(w, a, 1)[0] for w, a in zip(windows, arrived)]
    arrived = [exchange(w, core) for w in windows]
    half = windows[0].shape[0]

    plain = lambda count, parts: jax.ShapeDtypeStruct((count, parts * (part + 2 * HDIM)), jnp.float32)
    code = lambda count, parts: jax.ShapeDtypeStruct((count, parts * (part + 3 * HDIM)), jnp.bfloat16)

    def attend(chain):
        return call(
            functools.partial(attend_kernel, first_head=chain * part // HDIM),
            (plain(half, 1), plain(half, 1)),
            (windows[chain], arrived[chain], keys, values),
            8 * half * tokens * part,
            [pltpu.VMEM((4, 2 * half, tokens), jnp.float32), pltpu.VMEM((4, 4 * half, tokens), jnp.bfloat16)],
            16 << 20,
        )

    def merge(sources, kinds, count, chains):
        kernel = functools.partial(merge_kernel, kinds=kinds, chains=chains)
        shapes = (plain(count, chains), code(count, chains))
        return call(kernel, shapes, sources, 0, [pltpu.VMEM((count, part), jnp.float32)])

    parts = [attend(chain) for chain in range(CHAINS)]
    pairs = [(keep, exchange(send, core)) for keep, send in parts]
    kinds = ("sums", "sums")
    for mask in chips[:-1]:
        half = half // 2
        parts = [merge(pair, kinds, half, 1) for pair in pairs]
        pairs = [(keep, exchange(send, mask)) for keep, send in parts]
        kinds = ("means", "coded")
    keep, send = merge([array for pair in pairs for array in pair], kinds, half // 2, CHAINS)
    kernel = functools.partial(finish_kernel, kinds=("means", "coded"), chains=CHAINS)
    out = jax.ShapeDtypeStruct((rows, width), jnp.bfloat16)
    return call(kernel, out, (keep, exchange(send, chips[-1]), gain), 0)


def solution(mesh):
    spec = P(("grp", "seq"), None)
    return jax.shard_map(shards, mesh=mesh, in_specs=(spec, spec, spec, P()), out_specs=spec, check_vma=False)
```

```python
import functools
import math

import jax
import jax.numpy as jnp
from jax import lax
from jax.experimental import pallas as pl
from jax.experimental.pallas import tpu as pltpu
from jax.sharding import PartitionSpec as P

HDIM = 128
EXP2_SCALE = math.log2(math.e) / math.sqrt(HDIM)
FETCH_FLOPS = 1_500_000_000
CHAINS = 2
CODE_SPAN = 250.0
VMEM_SPEC = pl.BlockSpec(memory_space=pltpu.VMEM)


def copy_kernel(source_ref, out_ref):
    out_ref[...] = source_ref[...]


def join_kernel(here_ref, there_ref, *out_refs):
    for index, ref in enumerate(out_refs):
        width = ref.shape[1]
        columns = slice(index * width, (index + 1) * width)
        ref[...] = jnp.concatenate([here_ref[:, columns], there_ref[:, columns]], axis=0)


def attend_kernel(
    query_here_ref, query_there_ref, key_ref, value_ref, keep_ref, send_ref, dots_ref, weights_ref, *, first_head
):
    half, width = query_here_ref.shape
    rows = 2 * half
    heads = width // HDIM
    slots = dots_ref.shape[0]

    def shifted(head):
        return slice((first_head + head) * HDIM, (first_head + head + 1) * HDIM)

    def score(head):
        columns = slice(head * HDIM, (head + 1) * HDIM)
        dots_ref[head % slots] = lax.dot_general(
            jnp.concatenate([query_here_ref[:, columns], query_there_ref[:, columns]], axis=0),
            key_ref[:, shifted(head)],
            (((1,), (1,)), ((), ())),
            preferred_element_type=jnp.float32,
        )

    def weigh(head):
        dots = dots_ref[head % slots]
        peak = jnp.max(dots, axis=1, keepdims=True)
        weights = jnp.exp2((dots - peak) * EXP2_SCALE)
        total = jnp.sum(weights, axis=1, keepdims=True)
        coarse = weights.astype(jnp.bfloat16)
        weights_ref[head % slots, :rows] = coarse
        weights_ref[head % slots, rows:] = (weights - coarse.astype(jnp.float32)).astype(jnp.bfloat16)
        for ref, first in ((keep_ref, 0), (send_ref, half)):
            ref[:, width + head : width + head + 1] = peak[first : first + half]
            ref[:, width + HDIM + head : width + HDIM + head + 1] = total[first : first + half]

    def accumulate(head):
        columns = slice(head * HDIM, (head + 1) * HDIM)
        sums = jnp.dot(weights_ref[head % slots], value_ref[:, shifted(head)], preferred_element_type=jnp.float32)
        numerator = sums[:rows] + sums[rows:]
        keep_ref[:, columns] = numerator[:half]
        send_ref[:, columns] = numerator[half:]

    group = slots // 2
    for ref in (keep_ref, send_ref):
        ref[:, width:] = jnp.zeros((half, 2 * HDIM), jnp.float32)
    steps = heads // group
    for step in range(steps + 2):
        for member in range(group):
            for stage, lag in ((score, 0), (weigh, 1), (accumulate, 2)):
                if 0 <= step - lag < steps:
                    stage((step - lag) * group + member)


def exact_terms(values):
    first = values.astype(jnp.bfloat16).astype(jnp.float32)
    rest = values - first
    second = rest.astype(jnp.bfloat16).astype(jnp.float32)
    return first, second, rest - second


def pack_statistics(maxima, denominators, unit, heads):
    lane = lax.broadcasted_iota(jnp.int32, maxima.shape, 1)
    packed = unit
    for place, term in enumerate((*exact_terms(maxima), *exact_terms(denominators))):
        moved = term if place == 0 else pltpu.roll(term, place * heads, 1)
        packed = jnp.where((lane >= place * heads) & (lane < (place + 1) * heads), moved, packed)
    return packed.astype(jnp.bfloat16)


def unpack_statistics(packed, heads):
    terms = packed.astype(jnp.float32)
    place = [terms, *(pltpu.roll(terms, HDIM - index * heads, 1) for index in range(1, 6))]
    unit = jnp.broadcast_to(terms[:, 6 * heads : 6 * heads + 1], terms.shape)
    return place[0] + (place[1] + place[2]), place[3] + (place[4] + place[5]), unit


def read_statistics(ref, width, coded):
    if not coded:
        return ref[:, width : width + HDIM], ref[:, width + HDIM :], None
    maxima, denominators, unit = unpack_statistics(ref[:, width:], width // HDIM)
    return maxima, denominators, unit * (1.0 / CODE_SPAN)


def read_numerator(ref, columns, coded):
    if not coded:
        return ref[:, columns]
    code = ref[:, columns].astype(jnp.float32)
    size = jnp.log2(jnp.abs(code)) + CODE_SPAN / 2
    return jnp.where(code < 0, -size, size)


def combine(refs, coded, width):
    statistics = [read_statistics(ref, width, kind == "coded") for ref, kind in zip(refs, coded)]
    maxima = functools.reduce(jnp.maximum, [m for m, _, _ in statistics])
    scales = [jnp.exp2((m - maxima) * EXP2_SCALE) for m, _, _ in statistics]
    denominators = sum(scale * d for scale, (_, d, _) in zip(scales, statistics))
    inverse = 1.0 / denominators
    factors = []
    for kind, scale, (_, d, unit) in zip(coded, scales, statistics):
        factor = scale * inverse
        if kind != "sums":
            factor = factor * d
        factors.append(factor if unit is None else factor * unit)
    return maxima, denominators, factors


def combined_mean(refs, coded, factors, head):
    columns = slice(head * HDIM, (head + 1) * HDIM)
    lane = slice(head, head + 1)
    return sum(f[:, lane] * read_numerator(ref, columns, k == "coded") for ref, k, f in zip(refs, coded, factors))


def section(ref, index, width):
    return ref.at[:, index * width : (index + 1) * width]


def merge_kernel(*refs, kinds, chains):
    all_keep_ref, all_send_ref, means_ref = refs[2 * chains :]
    half, width = means_ref.shape
    heads = width // HDIM
    lane = lax.broadcasted_iota(jnp.int32, (half, HDIM), 1)
    for chain in range(chains):
        sources = refs[2 * chain : 2 * chain + 2]
        keep_ref = section(all_keep_ref, chain, width + 2 * HDIM)
        send_ref = section(all_send_ref, chain, width + HDIM)
        maxima, denominators, factors = combine(sources, kinds, width)
        largest = jnp.full((half, HDIM), 1e-30, jnp.float32)
        for head in range(heads):
            columns = slice(head * HDIM, (head + 1) * HDIM)
            merged = combined_mean(sources, kinds, factors, head)
            keep_ref[:, columns] = merged[:half]
            means_ref[:, columns] = merged[half:]
            largest = jnp.maximum(largest, jnp.abs(merged[half:]))
        unit = jnp.broadcast_to(jnp.max(largest, axis=1, keepdims=True), largest.shape)
        unit = (unit * 1.01).astype(jnp.bfloat16).astype(jnp.float32)
        step = CODE_SPAN / unit
        for head in range(heads):
            columns = slice(head * HDIM, (head + 1) * HDIM)
            mean = means_ref[:, columns]
            code = jnp.exp2(jnp.abs(mean) * step - CODE_SPAN / 2)
            send_ref[:, columns] = jnp.where(mean < 0, -code, code).astype(jnp.bfloat16)
        keep_ref[:, width : width + HDIM] = maxima[:half]
        keep_ref[:, width + HDIM :] = denominators[:half]
        send_ref[:, width:] = pack_statistics(maxima[half:], denominators[half:], unit, heads)


def finish_kernel(all_here_ref, all_there_ref, gain_ref, out_ref, *, kinds, chains):
    rows, all_width = out_ref.shape
    width = all_width // chains
    squares = jnp.zeros((rows, HDIM), jnp.float32)
    attended = []
    for chain in range(chains):
        sources = (section(all_here_ref, chain, width + 2 * HDIM), section(all_there_ref, chain, width + HDIM))
        _, _, factors = combine(sources, kinds, width)
        for head in range(width // HDIM):
            block = combined_mean(sources, kinds, factors, head)
            squares = squares + block * block
            attended.append(block)
    mean = jnp.sum(squares, axis=1, keepdims=True) / all_width
    inverse = 1.0 / jnp.sqrt(mean + 1e-06)
    for head, block in enumerate(attended):
        columns = slice(head * HDIM, (head + 1) * HDIM)
        out_ref[:, columns] = (block * inverse * gain_ref[:, columns]).astype(out_ref.dtype)


def call(kernel, out_shape, operands, flops=0, scratch=(), limit=4 << 20):
    outs = out_shape if isinstance(out_shape, (tuple, list)) else [out_shape]
    size = sum(math.prod(a.shape) * a.dtype.itemsize for a in (*operands, *outs))
    return pl.pallas_call(
        kernel,
        out_shape=out_shape,
        in_specs=[VMEM_SPEC] * len(operands),
        out_specs=jax.tree.map(lambda _: VMEM_SPEC, out_shape),
        scratch_shapes=scratch,
        cost_estimate=pl.CostEstimate(flops=flops, bytes_accessed=size, transcendentals=0),
        compiler_params=pltpu.CompilerParams(vmem_limit_bytes=limit),
    )(*operands)


def exchange(array, mask):
    return lax.ppermute(array, "seq", [(i, i ^ mask) for i in range(lax.axis_size("seq"))])


def shards(queries, keys, values, gain):
    masks = [1 << bit for bit in range(lax.axis_size("seq").bit_length() - 1)]
    core, chips = masks[0], masks[1:]
    rows, width = queries.shape
    part = width // CHAINS
    tokens = keys.shape[0]
    gain = call(copy_kernel, jax.ShapeDtypeStruct((1, width), gain.dtype), [gain.reshape(1, width)], FETCH_FLOPS)

    def joined(window, arrived, parts):
        shape = jax.ShapeDtypeStruct((2 * window.shape[0], window.shape[1] // parts), window.dtype)
        return call(join_kernel, (shape,) * parts, [window, arrived], FETCH_FLOPS)

    windows = joined(queries, exchange(queries, chips[-1]), CHAINS)
    near = chips[:-1]
    orders = [near, near[1::-1] + near[2:]]
    for masks in list(zip(*orders))[::-1]:
        arrived = [exchange(w, m) for w, m in zip(windows, masks)]
        windows = [joined(w, a, 1)[0] for w, a in zip(windows, arrived)]
    arrived = [exchange(w, core) for w in windows]
    half = windows[0].shape[0]

    plain = lambda count, parts: jax.ShapeDtypeStruct((count, parts * (part + 2 * HDIM)), jnp.float32)
    code = lambda count, parts: jax.ShapeDtypeStruct((count, parts * (part + HDIM)), jnp.bfloat16)

    def attend(chain):
        return call(
            functools.partial(attend_kernel, first_head=chain * part // HDIM),
            (plain(half, 1), plain(half, 1)),
            (windows[chain], arrived[chain], keys, values),
            8 * half * tokens * part,
            [pltpu.VMEM((4, 2 * half, tokens), jnp.float32), pltpu.VMEM((4, 4 * half, tokens), jnp.bfloat16)],
            16 << 20,
        )

    def merge(sources, kinds, count, chains):
        kernel = functools.partial(merge_kernel, kinds=kinds, chains=chains)
        shapes = (plain(count, chains), code(count, chains))
        return call(kernel, shapes, sources, 0, [pltpu.VMEM((count, part), jnp.float32)])

    parts = [attend(chain) for chain in range(CHAINS)]
    pairs = [(keep, exchange(send, core)) for keep, send in parts]
    kinds = ("sums", "sums")
    for masks in zip(*orders):
        half = half // 2
        parts = [merge(pair, kinds, half, 1) for pair in pairs]
        pairs = [(k, exchange(s, m)) for (k, s), m in zip(parts, masks)]
        kinds = ("means", "coded")
    keep, send = merge([array for pair in pairs for array in pair], kinds, half // 2, CHAINS)
    kernel = functools.partial(finish_kernel, kinds=("means", "coded"), chains=CHAINS)
    out = jax.ShapeDtypeStruct((rows, width), jnp.bfloat16)
    return call(kernel, out, (keep, exchange(send, chips[-1]), gain), 0)


def solution(mesh):
    spec = P(("grp", "seq"), None)
    return jax.shard_map(shards, mesh=mesh, in_specs=(spec, spec, spec, P()), out_specs=spec, check_vma=False)
```

```python
import functools
import math

import jax
import jax.numpy as jnp
from jax import lax
from jax.experimental import pallas as pl
from jax.experimental.pallas import tpu as pltpu
from jax.sharding import PartitionSpec as P

HDIM = 128
EXP2_SCALE = math.log2(math.e) / math.sqrt(HDIM)
FETCH_FLOPS = 1_500_000_000
CHAINS = 2
CODE_SPAN = 250.0
VMEM_SPEC = pl.BlockSpec(memory_space=pltpu.VMEM)


def copy_kernel(source_ref, out_ref):
    out_ref[...] = source_ref[...]


def join_kernel(*refs):
    refs[-1][...] = jnp.concatenate([ref[...] for ref in refs[:-1]], axis=0)


def attend_kernel(
    query_here_ref, query_there_ref, key_ref, value_ref, keep_ref, send_ref, dots_ref, weights_ref, *, first_head
):
    half, width = query_here_ref.shape[0], keep_ref.shape[1] - 2 * HDIM
    rows = 2 * half
    heads = width // HDIM
    slots = dots_ref.shape[0]

    def shifted(head):
        return slice((first_head + head) * HDIM, (first_head + head + 1) * HDIM)

    def score(head):
        columns = shifted(head)
        dots_ref[head % slots] = lax.dot_general(
            jnp.concatenate([query_here_ref[:, columns], query_there_ref[:, columns]], axis=0),
            key_ref[:, columns],
            (((1,), (1,)), ((), ())),
            preferred_element_type=jnp.float32,
        )

    def weigh(head):
        dots = dots_ref[head % slots]
        peak = jnp.max(dots, axis=1, keepdims=True)
        weights = jnp.exp2((dots - peak) * EXP2_SCALE)
        total = jnp.sum(weights, axis=1, keepdims=True)
        coarse = weights.astype(jnp.bfloat16)
        weights_ref[head % slots, :rows] = coarse
        weights_ref[head % slots, rows:] = (weights - coarse.astype(jnp.float32)).astype(jnp.bfloat16)
        for ref, first in ((keep_ref, 0), (send_ref, half)):
            ref[:, width + head : width + head + 1] = peak[first : first + half]
            ref[:, width + HDIM + head : width + HDIM + head + 1] = total[first : first + half]

    def accumulate(head):
        columns = slice(head * HDIM, (head + 1) * HDIM)
        sums = jnp.dot(weights_ref[head % slots], value_ref[:, shifted(head)], preferred_element_type=jnp.float32)
        numerator = sums[:rows] + sums[rows:]
        keep_ref[:, columns] = numerator[:half]
        send_ref[:, columns] = numerator[half:]

    group = slots // 2
    for ref in (keep_ref, send_ref):
        ref[:, width:] = jnp.zeros((half, 2 * HDIM), jnp.float32)
    steps = heads // group
    for step in range(steps + 2):
        for member in range(group):
            for stage, lag in ((score, 0), (weigh, 1), (accumulate, 2)):
                if 0 <= step - lag < steps:
                    stage((step - lag) * group + member)


def exact_terms(values):
    first = values.astype(jnp.bfloat16).astype(jnp.float32)
    rest = values - first
    second = rest.astype(jnp.bfloat16).astype(jnp.float32)
    return first, second, rest - second


def pack_statistics(maxima, denominators, unit, heads):
    lane = lax.broadcasted_iota(jnp.int32, maxima.shape, 1)
    packed = unit
    for place, term in enumerate((*exact_terms(maxima), *exact_terms(denominators))):
        moved = term if place == 0 else pltpu.roll(term, place * heads, 1)
        packed = jnp.where((lane >= place * heads) & (lane < (place + 1) * heads), moved, packed)
    return packed.astype(jnp.bfloat16)


def unpack_statistics(packed, heads):
    terms = packed.astype(jnp.float32)
    place = [terms, *(pltpu.roll(terms, HDIM - index * heads, 1) for index in range(1, 6))]
    unit = jnp.broadcast_to(terms[:, 6 * heads : 6 * heads + 1], terms.shape)
    return place[0] + (place[1] + place[2]), place[3] + (place[4] + place[5]), unit


def read_statistics(ref, width, coded):
    if not coded:
        return ref[:, width : width + HDIM], ref[:, width + HDIM :], None
    maxima, denominators, unit = unpack_statistics(ref[:, width:], width // HDIM)
    return maxima, denominators, unit * (1.0 / CODE_SPAN)


def read_numerator(ref, columns, coded):
    if not coded:
        return ref[:, columns]
    code = ref[:, columns].astype(jnp.float32)
    size = jnp.log2(jnp.abs(code)) + CODE_SPAN / 2
    return jnp.where(code < 0, -size, size)


def combine(refs, coded, width):
    statistics = [read_statistics(ref, width, kind == "coded") for ref, kind in zip(refs, coded)]
    maxima = functools.reduce(jnp.maximum, [m for m, _, _ in statistics])
    scales = [jnp.exp2((m - maxima) * EXP2_SCALE) for m, _, _ in statistics]
    denominators = sum(scale * d for scale, (_, d, _) in zip(scales, statistics))
    inverse = 1.0 / denominators
    factors = []
    for kind, scale, (_, d, unit) in zip(coded, scales, statistics):
        factor = scale * inverse
        if kind != "sums":
            factor = factor * d
        factors.append(factor if unit is None else factor * unit)
    return maxima, denominators, factors


def combined_mean(refs, coded, factors, head):
    columns = slice(head * HDIM, (head + 1) * HDIM)
    lane = slice(head, head + 1)
    return sum(f[:, lane] * read_numerator(ref, columns, k == "coded") for ref, k, f in zip(refs, coded, factors))


def section(ref, chain, width, kind):
    stride = width + (HDIM if kind == "coded" else 2 * HDIM)
    return ref.at[:, chain * stride : (chain + 1) * stride]


def merge_kernel(*refs, kinds, chains, separate):
    count = len(kinds)
    arrays = count * chains if separate else count
    all_keep_ref, *all_send_refs = refs[arrays:-1]
    means_ref = refs[-1]
    block = all_keep_ref.shape[0]
    sent, width = means_ref.shape
    heads = width // HDIM
    for chain in range(chains):
        if separate:
            sources = refs[chain * count : (chain + 1) * count]
        else:
            sources = [section(ref, chain, width, kind) for ref, kind in zip(refs, kinds)]
        keep_ref = section(all_keep_ref, chain, width, "means")
        maxima, denominators, factors = combine(sources, kinds, width)
        largest = jnp.full((sent, HDIM), 1e-30, jnp.float32)
        for head in range(heads):
            columns = slice(head * HDIM, (head + 1) * HDIM)
            merged = combined_mean(sources, kinds, factors, head)
            keep_ref[:, columns] = merged[:block]
            means_ref[:, columns] = merged[block:]
            largest = jnp.maximum(largest, jnp.abs(merged[block:]))
        keep_ref[:, width : width + HDIM] = maxima[:block]
        keep_ref[:, width + HDIM :] = denominators[:block]
        unit = jnp.broadcast_to(jnp.max(largest, axis=1, keepdims=True), largest.shape)
        unit = (unit * 1.01).astype(jnp.bfloat16).astype(jnp.float32)
        step = CODE_SPAN / unit
        statistics = pack_statistics(maxima[block:], denominators[block:], unit, heads)
        for index, all_send_ref in enumerate(all_send_refs):
            rows = slice(index * block, (index + 1) * block)
            send_ref = section(all_send_ref, chain, width, "coded")
            send_ref[:, width:] = statistics[rows]
            for head in range(heads):
                columns = slice(head * HDIM, (head + 1) * HDIM)
                mean = means_ref[rows, columns]
                code = jnp.exp2(jnp.abs(mean) * step[rows] - CODE_SPAN / 2)
                send_ref[:, columns] = jnp.where(mean < 0, -code, code).astype(jnp.bfloat16)


def finish_kernel(*refs, kinds, chains):
    gain_ref, out_ref = refs[-2:]
    rows, all_width = out_ref.shape
    width = all_width // chains
    squares = jnp.zeros((rows, HDIM), jnp.float32)
    attended = []
    for chain in range(chains):
        sources = [section(ref, chain, width, kind) for ref, kind in zip(refs, kinds)]
        _, _, factors = combine(sources, kinds, width)
        for head in range(width // HDIM):
            block = combined_mean(sources, kinds, factors, head)
            squares = squares + block * block
            attended.append(block)
    mean = jnp.sum(squares, axis=1, keepdims=True) / all_width
    inverse = 1.0 / jnp.sqrt(mean + 1e-06)
    for head, block in enumerate(attended):
        columns = slice(head * HDIM, (head + 1) * HDIM)
        out_ref[:, columns] = (block * inverse * gain_ref[:, columns]).astype(out_ref.dtype)


def call(kernel, out_shape, operands, flops=0, scratch=(), limit=4 << 20):
    outs = out_shape if isinstance(out_shape, (tuple, list)) else [out_shape]
    size = sum(math.prod(a.shape) * a.dtype.itemsize for a in (*operands, *outs))
    return pl.pallas_call(
        kernel,
        out_shape=out_shape,
        in_specs=[VMEM_SPEC] * len(operands),
        out_specs=jax.tree.map(lambda _: VMEM_SPEC, out_shape),
        scratch_shapes=scratch,
        cost_estimate=pl.CostEstimate(flops=flops, bytes_accessed=size, transcendentals=0),
        compiler_params=pltpu.CompilerParams(vmem_limit_bytes=limit),
    )(*operands)


def exchange(array, mask):
    return lax.ppermute(array, "seq", [(i, i ^ mask) for i in range(lax.axis_size("seq"))])


def chip_stages(peers):
    bits = [1 << bit for bit in range(1, peers.bit_length() - 1)]
    square = [bits[:1], [*bits[:2], sum(bits[:2])]][len(bits) > 2]
    return [[mask ^ 1 for mask in masks] for masks in (square, *([bit] for bit in bits[len(square).bit_length() :]))]


def shards(queries, keys, values, gain):
    stages = chip_stages(lax.axis_size("seq"))
    core = 1
    rows, width = queries.shape
    part = width // CHAINS
    tokens = keys.shape[0]
    gain = call(copy_kernel, jax.ShapeDtypeStruct((1, width), gain.dtype), [gain.reshape(1, width)], FETCH_FLOPS)

    window = queries
    for masks in reversed(stages):
        pieces = [window, *(exchange(window, mask) for mask in masks)]
        shape = jax.ShapeDtypeStruct((len(pieces) * window.shape[0], width), window.dtype)
        window = call(join_kernel, shape, pieces, FETCH_FLOPS)
    arrived = exchange(window, core)
    count = window.shape[0]

    plain = lambda count, parts: jax.ShapeDtypeStruct((count, parts * (part + 2 * HDIM)), jnp.float32)
    code = lambda count: jax.ShapeDtypeStruct((count, CHAINS * (part + HDIM)), jnp.bfloat16)

    sources = []
    for chain in range(CHAINS):
        keep, send = call(
            functools.partial(attend_kernel, first_head=chain * part // HDIM),
            (plain(count, 1), plain(count, 1)),
            (window, arrived, keys, values),
            8 * count * tokens * part,
            [pltpu.VMEM((4, 2 * count, tokens), jnp.float32), pltpu.VMEM((4, 4 * count, tokens), jnp.bfloat16)],
            16 << 20,
        )
        sources += [keep, exchange(send, core)]
    kinds, separate = ("sums", "sums"), True
    for masks in stages:
        block = count // (len(masks) + 1)
        keep, *sends = call(
            functools.partial(merge_kernel, kinds=kinds, chains=CHAINS, separate=separate),
            (plain(block, CHAINS), *[code(block)] * len(masks)),
            sources,
            0,
            [pltpu.VMEM((count - block, part), jnp.float32)],
        )
        sources = [keep, *(exchange(send, mask) for send, mask in zip(sends, masks))]
        kinds, separate, count = ("means", *["coded"] * len(masks)), False, block
    kernel = functools.partial(finish_kernel, kinds=kinds, chains=CHAINS)
    return call(kernel, jax.ShapeDtypeStruct((rows, width), jnp.bfloat16), (*sources, gain), 0)


def solution(mesh):
    spec = P(("grp", "seq"), None)
    return jax.shard_map(shards, mesh=mesh, in_specs=(spec, spec, spec, P()), out_specs=spec, check_vma=False)
```

```python
import functools
import math

import jax
import jax.numpy as jnp
from jax import lax
from jax.experimental import pallas as pl
from jax.experimental.pallas import tpu as pltpu
from jax.sharding import PartitionSpec as P

HDIM = 128
EXP2_SCALE = math.log2(math.e) / math.sqrt(HDIM)
FETCH_FLOPS = 1_500_000_000
CHAINS = 2
CODE_SPAN = 250.0
VMEM_SPEC = pl.BlockSpec(memory_space=pltpu.VMEM)


def copy_kernel(source_ref, out_ref):
    out_ref[...] = source_ref[...]


def join_kernel(*refs):
    refs[-1][...] = jnp.concatenate([ref[...] for ref in refs[:-1]], axis=0)


def attend_kernel(
    query_here_ref, query_there_ref, key_ref, value_ref, keep_ref, send_ref, dots_ref, weights_ref, *, first_head
):
    half, width = query_here_ref.shape[0], keep_ref.shape[1] - 2 * HDIM
    rows = 2 * half
    heads = width // HDIM
    slots = dots_ref.shape[0]

    def shifted(head):
        return slice((first_head + head) * HDIM, (first_head + head + 1) * HDIM)

    def score(head):
        columns = shifted(head)
        dots_ref[head % slots] = lax.dot_general(
            jnp.concatenate([query_here_ref[:, columns], query_there_ref[:, columns]], axis=0),
            key_ref[:, columns],
            (((1,), (1,)), ((), ())),
            preferred_element_type=jnp.float32,
        )

    def weigh(head):
        dots = dots_ref[head % slots]
        peak = jnp.max(dots, axis=1, keepdims=True)
        weights = jnp.exp2((dots - peak) * EXP2_SCALE)
        total = jnp.sum(weights, axis=1, keepdims=True)
        coarse = weights.astype(jnp.bfloat16)
        weights_ref[head % slots, :rows] = coarse
        weights_ref[head % slots, rows:] = (weights - coarse.astype(jnp.float32)).astype(jnp.bfloat16)
        for ref, first in ((keep_ref, 0), (send_ref, half)):
            ref[:, width + head : width + head + 1] = peak[first : first + half]
            ref[:, width + HDIM + head : width + HDIM + head + 1] = total[first : first + half]

    def accumulate(head):
        columns = slice(head * HDIM, (head + 1) * HDIM)
        sums = jnp.dot(weights_ref[head % slots], value_ref[:, shifted(head)], preferred_element_type=jnp.float32)
        numerator = sums[:rows] + sums[rows:]
        keep_ref[:, columns] = numerator[:half]
        send_ref[:, columns] = numerator[half:]

    group = slots // 2
    for ref in (keep_ref, send_ref):
        ref[:, width:] = jnp.zeros((half, 2 * HDIM), jnp.float32)
    steps = heads // group
    for step in range(steps + 2):
        for member in range(group):
            for stage, lag in ((score, 0), (weigh, 1), (accumulate, 2)):
                if 0 <= step - lag < steps:
                    stage((step - lag) * group + member)


def exact_terms(values):
    first = values.astype(jnp.bfloat16).astype(jnp.float32)
    rest = values - first
    second = rest.astype(jnp.bfloat16).astype(jnp.float32)
    return first, second, rest - second


def pack_statistics(maxima, denominators, unit, heads):
    lane = lax.broadcasted_iota(jnp.int32, maxima.shape, 1)
    packed = unit
    for place, term in enumerate((*exact_terms(maxima), *exact_terms(denominators))):
        moved = term if place == 0 else pltpu.roll(term, place * heads, 1)
        packed = jnp.where((lane >= place * heads) & (lane < (place + 1) * heads), moved, packed)
    return packed.astype(jnp.bfloat16)


def unpack_statistics(packed, heads):
    terms = packed.astype(jnp.float32)
    place = [terms, *(pltpu.roll(terms, HDIM - index * heads, 1) for index in range(1, 6))]
    unit = jnp.broadcast_to(terms[:, 6 * heads : 6 * heads + 1], terms.shape)
    return place[0] + (place[1] + place[2]), place[3] + (place[4] + place[5]), unit


def read_statistics(ref, width, coded):
    if not coded:
        return ref[:, width : width + HDIM], ref[:, width + HDIM :], None
    maxima, denominators, unit = unpack_statistics(ref[:, width:], width // HDIM)
    return maxima, denominators, unit * (1.0 / CODE_SPAN)


def read_numerator(ref, columns, coded):
    if not coded:
        return ref[:, columns]
    code = ref[:, columns].astype(jnp.float32)
    size = jnp.log2(jnp.abs(code)) + CODE_SPAN / 2
    return jnp.where(code < 0, -size, size)


def combine(refs, coded, width):
    statistics = [read_statistics(ref, width, kind == "coded") for ref, kind in zip(refs, coded)]
    maxima = functools.reduce(jnp.maximum, [m for m, _, _ in statistics])
    scales = [jnp.exp2((m - maxima) * EXP2_SCALE) for m, _, _ in statistics]
    denominators = sum(scale * d for scale, (_, d, _) in zip(scales, statistics))
    inverse = 1.0 / denominators
    factors = []
    for kind, scale, (_, d, unit) in zip(coded, scales, statistics):
        factor = scale * inverse
        if kind != "sums":
            factor = factor * d
        factors.append(factor if unit is None else factor * unit)
    return maxima, denominators, factors


def combined_mean(refs, coded, factors, head):
    columns = slice(head * HDIM, (head + 1) * HDIM)
    lane = slice(head, head + 1)
    return sum(f[:, lane] * read_numerator(ref, columns, k == "coded") for ref, k, f in zip(refs, coded, factors))


def section(ref, chain, width, kind):
    stride = width + (HDIM if kind == "coded" else 2 * HDIM)
    return ref.at[:, chain * stride : (chain + 1) * stride]


def merge_kernel(*refs, kinds, chains, results):
    all_keep_ref, *all_send_refs = refs[-1 - results : -1]
    means_ref = refs[-1]
    block = all_keep_ref.shape[0]
    sent, width = means_ref.shape[0], means_ref.shape[1] // len(chains)
    heads = width // HDIM
    sources = [[section(ref, i, width, k) for ref, k in zip(refs, kinds)] for i in range(len(chains))]
    keeps = [section(all_keep_ref, chain, width, "means") for chain in chains]
    combined = [combine(group, kinds, width) for group in sources]
    steps = []
    for index, (group, keep_ref, (maxima, denominators, factors)) in enumerate(zip(sources, keeps, combined)):
        largest = jnp.full((sent, HDIM), 1e-30, jnp.float32)
        for head in range(heads):
            columns = slice(head * HDIM, (head + 1) * HDIM)
            merged = combined_mean(group, kinds, factors, head)
            keep_ref[:, columns] = merged[:block]
            means_ref[:, index * width + head * HDIM : index * width + (head + 1) * HDIM] = merged[block:]
            largest = jnp.maximum(largest, jnp.abs(merged[block:]))
        keep_ref[:, width : width + HDIM] = maxima[:block]
        keep_ref[:, width + HDIM :] = denominators[:block]
        unit = jnp.broadcast_to(jnp.max(largest, axis=1, keepdims=True), largest.shape)
        unit = (unit * 1.01).astype(jnp.bfloat16).astype(jnp.float32)
        steps.append((CODE_SPAN / unit, pack_statistics(maxima[block:], denominators[block:], unit, heads)))
    for index, (chain, (step, statistics)) in enumerate(zip(chains, steps)):
        for place, all_send_ref in enumerate(all_send_refs):
            rows = slice(place * block, (place + 1) * block)
            send_ref = section(all_send_ref, chain, width, "coded")
            send_ref[:, width:] = statistics[rows]
            for head in range(heads):
                columns = slice(head * HDIM, (head + 1) * HDIM)
                mean = means_ref[rows, index * width + head * HDIM : index * width + (head + 1) * HDIM]
                code = jnp.exp2(jnp.abs(mean) * step[rows] - CODE_SPAN / 2)
                send_ref[:, columns] = jnp.where(mean < 0, -code, code).astype(jnp.bfloat16)


def finish_kernel(*refs, kinds, chains):
    gain_ref, out_ref = refs[-2:]
    rows, all_width = out_ref.shape
    width = all_width // chains
    sources = [[section(ref, chain, width, k) for ref, k in zip(refs, kinds)] for chain in range(chains)]
    combined = [combine(group, kinds, width) for group in sources]
    squares = [jnp.zeros((rows, HDIM), jnp.float32)] * 4
    attended = []
    for group, (_, _, factors) in zip(sources, combined):
        for head in range(width // HDIM):
            block = combined_mean(group, kinds, factors, head)
            squares[head % 4] = squares[head % 4] + block * block
            attended.append(block)
    squares = sum(squares)
    mean = jnp.sum(squares, axis=1, keepdims=True) / all_width
    inverse = 1.0 / jnp.sqrt(mean + 1e-06)
    for head, block in enumerate(attended):
        columns = slice(head * HDIM, (head + 1) * HDIM)
        out_ref[:, columns] = (block * inverse * gain_ref[:, columns]).astype(out_ref.dtype)


def call(kernel, out_shape, operands, flops=0, scratch=(), limit=4 << 20, aliases={}):
    outs = out_shape if isinstance(out_shape, (tuple, list)) else [out_shape]
    size = sum(math.prod(a.shape) * a.dtype.itemsize for a in (*operands, *outs))
    return pl.pallas_call(
        kernel,
        out_shape=out_shape,
        in_specs=[VMEM_SPEC] * len(operands),
        out_specs=jax.tree.map(lambda _: VMEM_SPEC, out_shape),
        scratch_shapes=scratch,
        input_output_aliases=aliases,
        cost_estimate=pl.CostEstimate(flops=flops, bytes_accessed=size, transcendentals=0),
        compiler_params=pltpu.CompilerParams(vmem_limit_bytes=limit),
    )(*operands)


def exchange(array, mask):
    return lax.ppermute(array, "seq", [(i, i ^ mask) for i in range(lax.axis_size("seq"))])


def chip_stages(peers):
    bits = [1 << bit for bit in range(1, peers.bit_length() - 1)]
    square = [bits[:1], [sum(bits[:2]), *bits[:2]]][len(bits) > 2]
    return [square, *([bit] for bit in bits[len(square).bit_length() :])]


def shards(queries, keys, values, gain):
    stages = chip_stages(lax.axis_size("seq"))
    core = 1
    rows, width = queries.shape
    part = width // CHAINS
    tokens = keys.shape[0]
    gain = call(copy_kernel, jax.ShapeDtypeStruct((1, width), gain.dtype), [gain.reshape(1, width)], FETCH_FLOPS)

    window = queries
    for masks in reversed(stages):
        pieces = [window, *(exchange(window, mask) for mask in masks)]
        shape = jax.ShapeDtypeStruct((len(pieces) * window.shape[0], width), window.dtype)
        window = call(join_kernel, shape, pieces, FETCH_FLOPS)
    arrived = exchange(window, core)
    count = window.shape[0]

    plain = lambda count, parts: jax.ShapeDtypeStruct((count, parts * (part + 2 * HDIM)), jnp.float32)
    code = lambda count: jax.ShapeDtypeStruct((count, CHAINS * (part + HDIM)), jnp.bfloat16)

    def merge(sources, kinds, masks, block, chains, before):
        shapes = (plain(block, CHAINS), *[code(block)] * len(masks))
        return call(
            functools.partial(merge_kernel, kinds=kinds, chains=chains, results=len(shapes)),
            shapes,
            (*sources, *before),
            0,
            [pltpu.VMEM((block * len(masks), part * len(chains)), jnp.float32)],
            aliases={len(sources) + place: place for place in range(len(before))},
        )

    partials = []
    for chain in range(CHAINS):
        keep, send = call(
            functools.partial(attend_kernel, first_head=chain * part // HDIM),
            (plain(count, 1), plain(count, 1)),
            (window, arrived, keys, values),
            8 * count * tokens * part,
            [pltpu.VMEM((4, 2 * count, tokens), jnp.float32), pltpu.VMEM((4, 4 * count, tokens), jnp.bfloat16)],
            16 << 20,
        )
        partials.append((keep, exchange(send, core)))
    for masks in stages:
        count = count // (len(masks) + 1)
        if partials is not None:
            merged = ()
            for chain, pair in enumerate(partials):
                merged = merge(pair, ("sums", "sums"), masks, count, (chain,), merged)
            partials = None
        else:
            merged = merge(sources, kinds, masks, count, tuple(range(CHAINS)), ())
        keep, *sends = merged
        sources = [keep, *(exchange(send, mask) for send, mask in zip(sends, masks))]
        kinds = ("means", *["coded"] * len(masks))
    kernel = functools.partial(finish_kernel, kinds=kinds, chains=CHAINS)
    return call(kernel, jax.ShapeDtypeStruct((rows, width), jnp.bfloat16), (*sources, gain), 0)


def solution(mesh):
    spec = P(("grp", "seq"), None)
    return jax.shard_map(shards, mesh=mesh, in_specs=(spec, spec, spec, P()), out_specs=spec, check_vma=False)
```

```python
import functools
import math

import jax
import jax.numpy as jnp
from jax import lax
from jax.experimental import pallas as pl
from jax.experimental.pallas import tpu as pltpu
from jax.sharding import PartitionSpec as P

HDIM = 128
EXP2_SCALE = math.log2(math.e) / math.sqrt(HDIM)
FETCH_FLOPS = 1_500_000_000
CHAINS = 2
CODE_SPAN = 250.0
VMEM_SPEC = pl.BlockSpec(memory_space=pltpu.VMEM)


def copy_kernel(source_ref, out_ref):
    out_ref[...] = source_ref[...]


def join_kernel(*refs, count):
    first = 0
    for out_ref in refs[count:]:
        columns = slice(first, first + out_ref.shape[1])
        out_ref[...] = jnp.concatenate([ref[:, columns] for ref in refs[:count]], axis=0)
        first = columns.stop


def attend_kernel(
    query_here_ref, query_there_ref, key_ref, value_ref, keep_ref, send_ref, dots_ref, weights_ref, *, first_head
):
    half, width = query_here_ref.shape[0], keep_ref.shape[1] - 2 * HDIM
    rows = 2 * half
    heads = width // HDIM
    slots = dots_ref.shape[0]

    def shifted(head):
        return slice((first_head + head) * HDIM, (first_head + head + 1) * HDIM)

    def score(head):
        columns = slice(head * HDIM, (head + 1) * HDIM)
        dots_ref[head % slots] = lax.dot_general(
            jnp.concatenate([query_here_ref[:, columns], query_there_ref[:, columns]], axis=0),
            key_ref[:, shifted(head)],
            (((1,), (1,)), ((), ())),
            preferred_element_type=jnp.float32,
        )

    def weigh(head):
        dots = dots_ref[head % slots]
        peak = jnp.max(dots, axis=1, keepdims=True)
        weights = jnp.exp2((dots - peak) * EXP2_SCALE)
        total = jnp.sum(weights, axis=1, keepdims=True)
        coarse = weights.astype(jnp.bfloat16)
        weights_ref[head % slots, :rows] = coarse
        weights_ref[head % slots, rows:] = (weights - coarse.astype(jnp.float32)).astype(jnp.bfloat16)
        for ref, first in ((keep_ref, 0), (send_ref, half)):
            ref[:, width + head : width + head + 1] = peak[first : first + half]
            ref[:, width + HDIM + head : width + HDIM + head + 1] = total[first : first + half]

    def accumulate(head):
        columns = slice(head * HDIM, (head + 1) * HDIM)
        sums = jnp.dot(weights_ref[head % slots], value_ref[:, shifted(head)], preferred_element_type=jnp.float32)
        numerator = sums[:rows] + sums[rows:]
        keep_ref[:, columns] = numerator[:half]
        send_ref[:, columns] = numerator[half:]

    group = slots // 2
    for ref in (keep_ref, send_ref):
        ref[:, width:] = jnp.zeros((half, 2 * HDIM), jnp.float32)
    steps = heads // group
    for step in range(steps + 2):
        for member in range(group):
            for stage, lag in ((score, 0), (weigh, 1), (accumulate, 2)):
                if 0 <= step - lag < steps:
                    stage((step - lag) * group + member)


def exact_terms(values):
    first = values.astype(jnp.bfloat16).astype(jnp.float32)
    rest = values - first
    second = rest.astype(jnp.bfloat16).astype(jnp.float32)
    return first, second, rest - second


def pack_statistics(maxima, denominators, unit, heads):
    lane = lax.broadcasted_iota(jnp.int32, maxima.shape, 1)
    packed = unit
    for place, term in enumerate((*exact_terms(maxima), *exact_terms(denominators))):
        moved = term if place == 0 else pltpu.roll(term, place * heads, 1)
        packed = jnp.where((lane >= place * heads) & (lane < (place + 1) * heads), moved, packed)
    return packed.astype(jnp.bfloat16)


def unpack_statistics(packed, heads):
    terms = packed.astype(jnp.float32)
    place = [terms, *(pltpu.roll(terms, HDIM - index * heads, 1) for index in range(1, 6))]
    unit = jnp.broadcast_to(terms[:, 6 * heads : 6 * heads + 1], terms.shape)
    return place[0] + (place[1] + place[2]), place[3] + (place[4] + place[5]), unit


def read_statistics(ref, width, coded):
    if not coded:
        return ref[:, width : width + HDIM], ref[:, width + HDIM :], None
    maxima, denominators, unit = unpack_statistics(ref[:, width:], width // HDIM)
    return maxima, denominators, unit * (1.0 / CODE_SPAN)


def read_numerator(ref, columns, coded):
    if not coded:
        return ref[:, columns]
    code = ref[:, columns].astype(jnp.float32)
    size = jnp.log2(jnp.abs(code)) + CODE_SPAN / 2
    return jnp.where(code < 0, -size, size)


def combine(refs, coded, width):
    statistics = [read_statistics(ref, width, kind == "coded") for ref, kind in zip(refs, coded)]
    maxima = functools.reduce(jnp.maximum, [m for m, _, _ in statistics])
    scales = [jnp.exp2((m - maxima) * EXP2_SCALE) for m, _, _ in statistics]
    denominators = sum(scale * d for scale, (_, d, _) in zip(scales, statistics))
    inverse = 1.0 / denominators
    factors = []
    for kind, scale, (_, d, unit) in zip(coded, scales, statistics):
        factor = scale * inverse
        if kind != "sums":
            factor = factor * d
        factors.append(factor if unit is None else factor * unit)
    return maxima, denominators, factors


def combined_mean(refs, coded, factors, head):
    columns = slice(head * HDIM, (head + 1) * HDIM)
    lane = slice(head, head + 1)
    return sum(f[:, lane] * read_numerator(ref, columns, k == "coded") for ref, k, f in zip(refs, coded, factors))


def section(ref, chain, width, kind):
    stride = width + (HDIM if kind == "coded" else 2 * HDIM)
    return ref.at[:, chain * stride : (chain + 1) * stride]


def merge_kernel(*refs, kinds, chains, results):
    all_keep_ref, *all_send_refs = refs[-1 - results : -1]
    means_ref = refs[-1]
    block = all_keep_ref.shape[0]
    sent, width = means_ref.shape[0], means_ref.shape[1] // len(chains)
    heads = width // HDIM
    sources = [[section(ref, i, width, k) for ref, k in zip(refs, kinds)] for i in range(len(chains))]
    keeps = [section(all_keep_ref, chain, width, "means") for chain in chains]
    combined = [combine(group, kinds, width) for group in sources]
    steps = []
    for index, (group, keep_ref, (maxima, denominators, factors)) in enumerate(zip(sources, keeps, combined)):
        largest = jnp.full((sent, HDIM), 1e-30, jnp.float32)
        for head in range(heads):
            columns = slice(head * HDIM, (head + 1) * HDIM)
            merged = combined_mean(group, kinds, factors, head)
            keep_ref[:, columns] = merged[:block]
            means_ref[:, index * width + head * HDIM : index * width + (head + 1) * HDIM] = merged[block:]
            largest = jnp.maximum(largest, jnp.abs(merged[block:]))
        keep_ref[:, width : width + HDIM] = maxima[:block]
        keep_ref[:, width + HDIM :] = denominators[:block]
        unit = jnp.broadcast_to(jnp.max(largest, axis=1, keepdims=True), largest.shape)
        unit = (unit * 1.01).astype(jnp.bfloat16).astype(jnp.float32)
        steps.append((CODE_SPAN / unit, pack_statistics(maxima[block:], denominators[block:], unit, heads)))
    for index, (chain, (step, statistics)) in enumerate(zip(chains, steps)):
        for place, all_send_ref in enumerate(all_send_refs):
            rows = slice(place * block, (place + 1) * block)
            send_ref = section(all_send_ref, chain, width, "coded")
            send_ref[:, width:] = statistics[rows]
            for head in range(heads):
                columns = slice(head * HDIM, (head + 1) * HDIM)
                mean = means_ref[rows, index * width + head * HDIM : index * width + (head + 1) * HDIM]
                code = jnp.exp2(jnp.abs(mean) * step[rows] - CODE_SPAN / 2)
                send_ref[:, columns] = jnp.where(mean < 0, -code, code).astype(jnp.bfloat16)


def finish_kernel(*refs, kinds, chains):
    gain_ref, out_ref = refs[-2:]
    rows, all_width = out_ref.shape
    width = all_width // chains
    sources = [[section(ref, chain, width, k) for ref, k in zip(refs, kinds)] for chain in range(chains)]
    combined = [combine(group, kinds, width) for group in sources]
    squares = [jnp.zeros((rows, HDIM), jnp.float32)] * 4
    attended = []
    for group, (_, _, factors) in zip(sources, combined):
        for head in range(width // HDIM):
            block = combined_mean(group, kinds, factors, head)
            squares[head % 4] = squares[head % 4] + block * block
            attended.append(block)
    squares = sum(squares)
    mean = jnp.sum(squares, axis=1, keepdims=True) / all_width
    inverse = 1.0 / jnp.sqrt(mean + 1e-06)
    for head, block in enumerate(attended):
        columns = slice(head * HDIM, (head + 1) * HDIM)
        out_ref[:, columns] = (block * inverse * gain_ref[:, columns]).astype(out_ref.dtype)


def call(kernel, out_shape, operands, flops=0, scratch=(), limit=4 << 20, aliases={}):
    outs = out_shape if isinstance(out_shape, (tuple, list)) else [out_shape]
    size = sum(math.prod(a.shape) * a.dtype.itemsize for a in (*operands, *outs))
    return pl.pallas_call(
        kernel,
        out_shape=out_shape,
        in_specs=[VMEM_SPEC] * len(operands),
        out_specs=jax.tree.map(lambda _: VMEM_SPEC, out_shape),
        scratch_shapes=scratch,
        input_output_aliases=aliases,
        cost_estimate=pl.CostEstimate(flops=flops, bytes_accessed=size, transcendentals=0),
        compiler_params=pltpu.CompilerParams(vmem_limit_bytes=limit),
    )(*operands)


def exchange(array, mask):
    return lax.ppermute(array, "seq", [(i, i ^ mask) for i in range(lax.axis_size("seq"))])


def chip_stages(peers):
    bits = [1 << bit for bit in range(1, peers.bit_length() - 1)]
    square = [bits[:1], [sum(bits[:2]), *bits[:2]]][len(bits) > 2]
    return [square, *([bit] for bit in bits[len(square).bit_length() :])]


def shards(queries, keys, values, gain):
    stages = chip_stages(lax.axis_size("seq"))
    core = 1
    rows, width = queries.shape
    part = width // CHAINS
    tokens = keys.shape[0]
    gain = call(copy_kernel, jax.ShapeDtypeStruct((1, width), gain.dtype), [gain.reshape(1, width)], FETCH_FLOPS)

    windows = [queries]
    for masks in reversed(stages):
        pieces = [windows[0], *(exchange(windows[0], mask) for mask in masks)]
        parts = CHAINS if masks is stages[0] else 1
        shape = jax.ShapeDtypeStruct((len(pieces) * windows[0].shape[0], width // parts), queries.dtype)
        kernel = functools.partial(join_kernel, count=len(pieces))
        windows = call(kernel, (shape,) * parts, pieces, FETCH_FLOPS)
    count = windows[0].shape[0]

    plain = lambda count, parts: jax.ShapeDtypeStruct((count, parts * (part + 2 * HDIM)), jnp.float32)
    code = lambda count: jax.ShapeDtypeStruct((count, CHAINS * (part + HDIM)), jnp.bfloat16)

    def merge(sources, kinds, masks, block, chains, before):
        shapes = (plain(block, CHAINS), *[code(block)] * len(masks))
        return call(
            functools.partial(merge_kernel, kinds=kinds, chains=chains, results=len(shapes)),
            shapes,
            (*sources, *before),
            0,
            [pltpu.VMEM((block * len(masks), part * len(chains)), jnp.float32)],
            aliases={len(sources) + place: place for place in range(len(before))},
        )

    partials = []
    for chain in range(CHAINS):
        keep, send = call(
            functools.partial(attend_kernel, first_head=chain * part // HDIM),
            (plain(count, 1), plain(count, 1)),
            (windows[chain], exchange(windows[chain], core), keys, values),
            8 * count * tokens * part,
            [pltpu.VMEM((4, 2 * count, tokens), jnp.float32), pltpu.VMEM((4, 4 * count, tokens), jnp.bfloat16)],
            16 << 20,
        )
        partials.append((keep, exchange(send, core)))
    for masks in stages:
        count = count // (len(masks) + 1)
        if partials is not None:
            merged = ()
            for chain, pair in enumerate(partials):
                merged = merge(pair, ("sums", "sums"), masks, count, (chain,), merged)
            partials = None
        else:
            merged = merge(sources, kinds, masks, count, tuple(range(CHAINS)), ())
        keep, *sends = merged
        sources = [keep, *(exchange(send, mask) for send, mask in zip(sends, masks))]
        kinds = ("means", *["coded"] * len(masks))
    kernel = functools.partial(finish_kernel, kinds=kinds, chains=CHAINS)
    return call(kernel, jax.ShapeDtypeStruct((rows, width), jnp.bfloat16), (*sources, gain), 0)


def solution(mesh):
    spec = P(("grp", "seq"), None)
    return jax.shard_map(shards, mesh=mesh, in_specs=(spec, spec, spec, P()), out_specs=spec, check_vma=False)
```

```python
import functools
import math

import jax
import jax.numpy as jnp
from jax import lax
from jax.experimental import pallas as pl
from jax.experimental.pallas import tpu as pltpu
from jax.sharding import PartitionSpec as P

HDIM = 128
EXP2_SCALE = math.log2(math.e) / math.sqrt(HDIM)
FETCH_FLOPS = 1_500_000_000
CHAINS = 2
CODE_SPAN = 250.0
VMEM_SPEC = pl.BlockSpec(memory_space=pltpu.VMEM)


def copy_kernel(source_ref, out_ref):
    out_ref[...] = source_ref[...]


def join_kernel(*refs, count):
    first = 0
    for out_ref in refs[count:]:
        columns = slice(first, first + out_ref.shape[1])
        out_ref[...] = jnp.concatenate([ref[:, columns] for ref in refs[:count]], axis=0)
        first = columns.stop


def attend_kernel(
    query_here_ref, query_there_ref, key_ref, value_ref, keep_ref, send_ref, dots_ref, weights_ref, *, first_head
):
    half, width = query_here_ref.shape[0], keep_ref.shape[1] - 2 * HDIM
    rows = 2 * half
    heads = width // HDIM
    slots = dots_ref.shape[0]

    def shifted(head):
        return slice((first_head + head) * HDIM, (first_head + head + 1) * HDIM)

    def score(head):
        columns = slice(head * HDIM, (head + 1) * HDIM)
        dots_ref[head % slots] = lax.dot_general(
            jnp.concatenate([query_here_ref[:, columns], query_there_ref[:, columns]], axis=0),
            key_ref[:, shifted(head)],
            (((1,), (1,)), ((), ())),
            preferred_element_type=jnp.float32,
        )

    def weigh(head):
        dots = dots_ref[head % slots]
        peak = jnp.max(dots, axis=1, keepdims=True)
        weights = jnp.exp2((dots - peak) * EXP2_SCALE)
        total = jnp.sum(weights, axis=1, keepdims=True)
        coarse = weights.astype(jnp.bfloat16)
        weights_ref[head % slots, :rows] = coarse
        weights_ref[head % slots, rows:] = (weights - coarse.astype(jnp.float32)).astype(jnp.bfloat16)
        for ref, first in ((keep_ref, 0), (send_ref, half)):
            ref[:, width + head : width + head + 1] = peak[first : first + half]
            ref[:, width + HDIM + head : width + HDIM + head + 1] = total[first : first + half]

    def accumulate(head):
        columns = slice(head * HDIM, (head + 1) * HDIM)
        sums = jnp.dot(weights_ref[head % slots], value_ref[:, shifted(head)], preferred_element_type=jnp.float32)
        numerator = sums[:rows] + sums[rows:]
        keep_ref[:, columns] = numerator[:half]
        send_ref[:, columns] = numerator[half:]

    group = slots // 2
    for ref in (keep_ref, send_ref):
        ref[:, width:] = jnp.zeros((half, 2 * HDIM), jnp.float32)
    steps = heads // group
    for step in range(steps + 2):
        for member in range(group):
            for stage, lag in ((score, 0), (weigh, 1), (accumulate, 2)):
                if 0 <= step - lag < steps:
                    stage((step - lag) * group + member)


def exact_terms(values):
    first = values.astype(jnp.bfloat16).astype(jnp.float32)
    rest = values - first
    second = rest.astype(jnp.bfloat16).astype(jnp.float32)
    return first, second, rest - second


def pack_statistics(maxima, denominators, unit, heads):
    lane = lax.broadcasted_iota(jnp.int32, maxima.shape, 1)
    packed = unit
    for place, term in enumerate((*exact_terms(maxima), *exact_terms(denominators))):
        moved = term if place == 0 else pltpu.roll(term, place * heads, 1)
        packed = jnp.where((lane >= place * heads) & (lane < (place + 1) * heads), moved, packed)
    return packed.astype(jnp.bfloat16)


def unpack_statistics(packed, heads):
    terms = packed.astype(jnp.float32)
    place = [terms, *(pltpu.roll(terms, HDIM - index * heads, 1) for index in range(1, 6))]
    unit = jnp.broadcast_to(terms[:, 6 * heads : 6 * heads + 1], terms.shape)
    return place[0] + (place[1] + place[2]), place[3] + (place[4] + place[5]), unit


def read_statistics(ref, width, coded):
    if not coded:
        return ref[:, width : width + HDIM], ref[:, width + HDIM :], None
    maxima, denominators, unit = unpack_statistics(ref[:, width:], width // HDIM)
    return maxima, denominators, unit * (1.0 / CODE_SPAN**2)


def read_numerator(ref, columns, coded):
    if not coded:
        return ref[:, columns]
    code = ref[:, columns].astype(jnp.float32)
    root = jnp.log2(jnp.abs(code)) + CODE_SPAN / 2
    return jnp.where(code < 0, -root, root) * root


def combine(refs, coded, width):
    statistics = [read_statistics(ref, width, kind == "coded") for ref, kind in zip(refs, coded)]
    maxima = functools.reduce(jnp.maximum, [m for m, _, _ in statistics])
    scales = [jnp.exp2((m - maxima) * EXP2_SCALE) for m, _, _ in statistics]
    denominators = sum(scale * d for scale, (_, d, _) in zip(scales, statistics))
    inverse = 1.0 / denominators
    factors = []
    for kind, scale, (_, d, unit) in zip(coded, scales, statistics):
        factor = scale * inverse
        if kind != "sums":
            factor = factor * d
        factors.append(factor if unit is None else factor * unit)
    return maxima, denominators, factors


def combined_mean(refs, coded, factors, head):
    columns = slice(head * HDIM, (head + 1) * HDIM)
    lane = slice(head, head + 1)
    return sum(f[:, lane] * read_numerator(ref, columns, k == "coded") for ref, k, f in zip(refs, coded, factors))


def section(ref, chain, width, kind):
    stride = width + (HDIM if kind == "coded" else 2 * HDIM)
    return ref.at[:, chain * stride : (chain + 1) * stride]


def merge_kernel(*refs, kinds, chains, results):
    all_keep_ref, *all_send_refs = refs[-1 - results : -1]
    means_ref = refs[-1]
    block = all_keep_ref.shape[0]
    sent, width = means_ref.shape[0], means_ref.shape[1] // len(chains)
    heads = width // HDIM
    sources = [[section(ref, i, width, k) for ref, k in zip(refs, kinds)] for i in range(len(chains))]
    keeps = [section(all_keep_ref, chain, width, "means") for chain in chains]
    combined = [combine(group, kinds, width) for group in sources]
    steps = []
    for index, (group, keep_ref, (maxima, denominators, factors)) in enumerate(zip(sources, keeps, combined)):
        largest = jnp.full((sent, HDIM), 1e-32, jnp.float32)
        for head in range(heads):
            columns = slice(head * HDIM, (head + 1) * HDIM)
            merged = combined_mean(group, kinds, factors, head)
            keep_ref[:, columns] = merged[:block]
            means_ref[:, index * width + head * HDIM : index * width + (head + 1) * HDIM] = merged[block:]
            largest = jnp.maximum(largest, jnp.abs(merged[block:]))
        keep_ref[:, width : width + HDIM] = maxima[:block]
        keep_ref[:, width + HDIM :] = denominators[:block]
        unit = jnp.broadcast_to(jnp.max(largest, axis=1, keepdims=True), largest.shape)
        unit = (unit * 1.01).astype(jnp.bfloat16).astype(jnp.float32)
        steps.append((CODE_SPAN**2 / unit, pack_statistics(maxima[block:], denominators[block:], unit, heads)))
    for index, (chain, (step, statistics)) in enumerate(zip(chains, steps)):
        for place, all_send_ref in enumerate(all_send_refs):
            rows = slice(place * block, (place + 1) * block)
            send_ref = section(all_send_ref, chain, width, "coded")
            send_ref[:, width:] = statistics[rows]
            for head in range(heads):
                columns = slice(head * HDIM, (head + 1) * HDIM)
                mean = means_ref[rows, index * width + head * HDIM : index * width + (head + 1) * HDIM]
                square = jnp.abs(mean) * step[rows]
                code = jnp.exp2(square * lax.rsqrt(jnp.maximum(square, 1e-30)) - CODE_SPAN / 2)
                send_ref[:, columns] = jnp.where(mean < 0, -code, code).astype(jnp.bfloat16)


def finish_kernel(*refs, kinds, chains):
    gain_ref, out_ref = refs[-2:]
    rows, all_width = out_ref.shape
    width = all_width // chains
    sources = [[section(ref, chain, width, k) for ref, k in zip(refs, kinds)] for chain in range(chains)]
    combined = [combine(group, kinds, width) for group in sources]
    squares = [jnp.zeros((rows, HDIM), jnp.float32)] * 4
    attended = []
    for group, (_, _, factors) in zip(sources, combined):
        for head in range(width // HDIM):
            block = combined_mean(group, kinds, factors, head)
            squares[head % 4] = squares[head % 4] + block * block
            attended.append(block)
    squares = sum(squares)
    mean = jnp.sum(squares, axis=1, keepdims=True) / all_width
    inverse = 1.0 / jnp.sqrt(mean + 1e-06)
    for head, block in enumerate(attended):
        columns = slice(head * HDIM, (head + 1) * HDIM)
        out_ref[:, columns] = (block * inverse * gain_ref[:, columns]).astype(out_ref.dtype)


def call(kernel, out_shape, operands, flops=0, scratch=(), limit=4 << 20, aliases={}):
    outs = out_shape if isinstance(out_shape, (tuple, list)) else [out_shape]
    size = sum(math.prod(a.shape) * a.dtype.itemsize for a in (*operands, *outs))
    return pl.pallas_call(
        kernel,
        out_shape=out_shape,
        in_specs=[VMEM_SPEC] * len(operands),
        out_specs=jax.tree.map(lambda _: VMEM_SPEC, out_shape),
        scratch_shapes=scratch,
        input_output_aliases=aliases,
        cost_estimate=pl.CostEstimate(flops=flops, bytes_accessed=size, transcendentals=0),
        compiler_params=pltpu.CompilerParams(vmem_limit_bytes=limit),
    )(*operands)


def exchange(array, mask):
    return lax.ppermute(array, "seq", [(i, i ^ mask) for i in range(lax.axis_size("seq"))])


def chip_stages(peers):
    bits = [1 << bit for bit in range(1, peers.bit_length() - 1)]
    square = [bits[:1], [bits[0], sum(bits[:2]), bits[1]]][len(bits) > 2]
    return [square, *([bit] for bit in bits[len(square).bit_length() :])]


def shards(queries, keys, values, gain):
    stages = chip_stages(lax.axis_size("seq"))
    core = 1
    rows, width = queries.shape
    part = width // CHAINS
    tokens = keys.shape[0]
    gain = call(copy_kernel, jax.ShapeDtypeStruct((1, width), gain.dtype), [gain.reshape(1, width)], FETCH_FLOPS)

    windows = [queries]
    for masks in reversed(stages):
        pieces = [windows[0], *(exchange(windows[0], mask) for mask in masks)]
        parts = CHAINS if masks is stages[0] else 1
        shape = jax.ShapeDtypeStruct((len(pieces) * windows[0].shape[0], width // parts), queries.dtype)
        kernel = functools.partial(join_kernel, count=len(pieces))
        windows = call(kernel, (shape,) * parts, pieces, FETCH_FLOPS)
    count = windows[0].shape[0]

    plain = lambda count, parts: jax.ShapeDtypeStruct((count, parts * (part + 2 * HDIM)), jnp.float32)
    code = lambda count: jax.ShapeDtypeStruct((count, CHAINS * (part + HDIM)), jnp.bfloat16)

    def merge(sources, kinds, masks, block, chains, before):
        shapes = (plain(block, CHAINS), *[code(block)] * len(masks))
        return call(
            functools.partial(merge_kernel, kinds=kinds, chains=chains, results=len(shapes)),
            shapes,
            (*sources, *before),
            0,
            [pltpu.VMEM((block * len(masks), part * len(chains)), jnp.float32)],
            aliases={len(sources) + place: place for place in range(len(before))},
        )

    partials = []
    for chain in range(CHAINS):
        keep, send = call(
            functools.partial(attend_kernel, first_head=chain * part // HDIM),
            (plain(count, 1), plain(count, 1)),
            (windows[chain], exchange(windows[chain], core), keys, values),
            8 * count * tokens * part,
            [pltpu.VMEM((4, 2 * count, tokens), jnp.float32), pltpu.VMEM((4, 4 * count, tokens), jnp.bfloat16)],
            16 << 20,
        )
        partials.append((keep, exchange(send, core)))
    for masks in stages:
        count = count // (len(masks) + 1)
        if partials is not None:
            merged = ()
            for chain, pair in enumerate(partials):
                merged = merge(pair, ("sums", "sums"), masks, count, (chain,), merged)
            partials = None
        else:
            merged = merge(sources, kinds, masks, count, tuple(range(CHAINS)), ())
        keep, *sends = merged
        sources = [keep, *(exchange(send, mask) for send, mask in zip(sends, masks))]
        kinds = ("means", *["coded"] * len(masks))
    kernel = functools.partial(finish_kernel, kinds=kinds, chains=CHAINS)
    return call(kernel, jax.ShapeDtypeStruct((rows, width), jnp.bfloat16), (*sources, gain), 0)


def solution(mesh):
    spec = P(("grp", "seq"), None)
    return jax.shard_map(shards, mesh=mesh, in_specs=(spec, spec, spec, P()), out_specs=spec, check_vma=False)
```
